256 devices in a mesh: sky: 32 (over z_hi, y, core), exp: 8 (over z_lo, x).
Axes of the slice: x: 4, y: 4, z: 8 (z_hi: 4, z_lo: 2; z = z_hi * 2 + z_lo), core: 2. Of those that a mesh axis runs over, the one named last changes fastest.
Arguments:
- warped: bfloat16 [16, 3840, 1024], P('exp', 'sky'), may hold values from -6 to 6
- variance: bfloat16 [16, 3840, 1024], P('exp', 'sky'), may hold values from 0.5 to 8
- basis_taps: bfloat16 [9, 2, 23], replicated, may hold values from -1.25 to 1.25
- coeffs: float32 [16, 9, 10], P('exp'), may hold values from -6 to 6
- degrees: int32 [16, 9], P('exp'), may hold values from 0 to 3
- footprint: int32 [16, 2], P('exp'), may hold values from 0 to 3840, as said below
- masks: int32 [16, 256], P('exp', 'sky'), may hold values from 0 to 1073741823
Outputs:
- coadd: float32 [3840, 1024], P('sky', 'exp')
The draws below stay inside these ranges and needn't reach their ends.
Inputs may be any that keep to these rules, and one draw needn't show every extreme that they name: Each exposure covers rows footprint[e, 0] up to but not including footprint[e, 1], a nonempty range.
All inputs are finite; a program needn't handle non-finite values.
Results may differ from the reference program's by a relative error of at most 0.0039.
Values may be sent and summed in bfloat16 or wider, within the bound.
A program may use at most 64 MiB of HBM per device.

```python
import math
import jax
import jax.numpy as jnp
from jax import lax

COLS = 1024
NB = 9
KW = 23
NTERM = 10
HALF = 11
NE = 16
NR = 3840


def draw_footprint(key, part):
    first_key, second_key = jax.random.split(jax.random.fold_in(key, 17))
    lower = jnp.maximum(jax.random.randint(first_key, (NE,), -(NR // 4), NR // 2), 0)
    upper = jnp.minimum(lower + jax.random.randint(second_key, (NE,), NR // 4, NR + 1), NR)
    return jnp.stack([lower, upper], axis=1).astype(jnp.int32)


def set_ends(result, rng, low, largest):
    longest = result.shape.index(max(result.shape))
    spots = []
    for shift in (0, 1):
        where = [jax.random.randint(jax.random.fold_in(rng, axis), (), 0, length) for axis, length in enumerate(result.shape)]
        where[longest] = (where[longest] + shift) % result.shape[longest]
        spots.append(tuple(where))
    return result.at[spots[0]].set(low).at[spots[1]].set(largest)


def level_of(key, extent, pieces, least, top_value):
    gain = 1.0
    for axis_at, blocks in pieces:
        heights = jax.random.uniform(jax.random.fold_in(jax.random.fold_in(key, 6), axis_at), (blocks,), jnp.float32, least / len(pieces), top_value / len(pieces))
        gain = gain * jnp.repeat(jnp.exp(heights), extent[axis_at] // blocks).reshape((-1,) + (1,) * (len(extent) - 1 - axis_at))
    return gain


def centred(stream_key, shape, deviation, reach, pieces=(), kind=jnp.bfloat16):
    result = deviation * jax.random.normal(stream_key, shape, jnp.float32)
    if pieces:
        result = result * level_of(stream_key, shape, pieces, -0.22, 0.18)
    return jnp.clip(result, -reach, reach).astype(kind)


def setup_inputs(seed: int = 0) -> dict:
    seeds = jax.random.split(jax.random.key(seed), 8)
    return {
        "warped": centred(seeds[0], (NE, NR, COLS), 1.0, 6.0, ((0, 8), (1, 32))),
        "variance": jnp.clip(jnp.exp(math.log(8.0) - 2.7725887 * jax.random.uniform(seeds[1], (NE, NR, COLS), jnp.float32) ** level_of(seeds[1], (NE, NR, COLS), ((0, 8), (1, 32)), -0.2, 0.2)), 0.5, 8.0).astype(jnp.bfloat16),
        "basis_taps": centred(seeds[2], (NB, 2, KW), KW ** -0.5, 1.25),
        "coeffs": centred(seeds[3], (NE, NB, NTERM), 0.4, 6.0, ((0, 8),), jnp.float32),
        "degrees": set_ends(jax.random.randint(seeds[4], (NE, NB), 0, 4), jax.random.fold_in(seeds[4], 1), 0, 3).astype(jnp.int32),
        "footprint": draw_footprint(jax.random.fold_in(seeds[7], 71), 0),
        "masks": set_ends(jax.random.randint(seeds[6], (NE, NR // 15), 0, 1073741824), jax.random.fold_in(seeds[6], 1), 0, 1073741823).astype(jnp.int32),
    }


HIGHEST = lax.Precision.HIGHEST
POWERS = ((0, 0), (1, 0), (0, 1), (2, 0), (1, 1), (0, 2), (3, 0), (2, 1), (1, 2), (0, 3))


def monomials(total_rows, total_cols, row_start, row_count):
    row_pos = (2.0 * (row_start + jnp.arange(row_count, dtype=jnp.int32)).astype(jnp.float32) + 1.0) / total_rows - 1.0
    col_pos = (2.0 * jnp.arange(total_cols, dtype=jnp.int32).astype(jnp.float32) + 1.0) / total_cols - 1.0
    return jnp.stack([(row_pos ** p)[:, None] * (col_pos ** q)[None, :] for p, q in POWERS])


def term_active(degree):
    orders = jnp.array([p + q for p, q in POWERS], dtype=jnp.int32)
    return (orders[None, :] <= degree[:, None]).astype(jnp.float32)


def pixel_weight(bounds, words, var_field, global_rows, local_rows):
    covered = ((global_rows >= bounds[0]) & (global_rows < bounds[1])).astype(jnp.float32)
    per_row = jnp.repeat(words, 15, total_repeat_length=local_rows.shape[0])
    offset = 2 * (local_rows % 15)
    lower = jnp.right_shift(per_row, offset) & 1
    upper = jnp.right_shift(per_row, offset + 1) & 1
    usable = (1 - lower * upper).astype(jnp.float32)
    return (covered * usable)[:, None] / var_field.astype(jnp.float32)


def reference(warped, variance, basis_taps, coeffs, degrees, footprint, masks):
    tap_values = basis_taps.astype(jnp.float32)
    row_kernel = tap_values[:, 0, :].reshape(NB, 1, KW, 1)
    col_kernel = tap_values[:, 1, :].reshape(NB, 1, 1, KW)
    terms_field = monomials(NR, COLS, 0, NR)
    row_index = jnp.arange(NR, dtype=jnp.int32)
    layout = ("NCHW", "OIHW", "NCHW")

    def first_pass(carry, item):
        image, coef, degree, bounds, words, var_field = item
        source = image.astype(jnp.float32).reshape(1, 1, NR, COLS)
        along_rows = lax.conv_general_dilated(source, row_kernel, (1, 1), ((HALF, HALF), (0, 0)), dimension_numbers=layout, precision=HIGHEST)
        along_rows = lax.optimization_barrier(along_rows.astype(jnp.bfloat16)).astype(jnp.float32)
        along_cols = lax.conv_general_dilated(along_rows, col_kernel, (1, 1), ((0, 0), (HALF, HALF)), dimension_numbers=layout, feature_group_count=NB, precision=HIGHEST)[0]
        field = jnp.einsum("bt,trc->brc", coef * term_active(degree), terms_field, precision=HIGHEST)
        matched = jnp.sum(field * along_cols, axis=0).astype(jnp.bfloat16)
        weight = pixel_weight(bounds, words, var_field, row_index, row_index)
        values = matched.astype(jnp.float32)
        return (carry[0] + weight * values, carry[1] + weight), matched

    start = (jnp.zeros((NR, COLS), jnp.float32), jnp.zeros((NR, COLS), jnp.float32))
    (num_first, den_first), matched_all = lax.scan(first_pass, start, (warped, coeffs, degrees, footprint, masks, variance))
    first = num_first / (1.0 + den_first)

    def second_pass(carry, item):
        matched, bounds, words, var_field = item
        weight = pixel_weight(bounds, words, var_field, row_index, row_index)
        values = matched.astype(jnp.float32)
        excess = values - first
        robust = weight / (1.0 + excess * excess / (9.0 * var_field.astype(jnp.float32)))
        return (carry[0] + robust * values, carry[1] + robust), None

    (num_final, den_final), unused = lax.scan(second_pass, start, (matched_all, footprint, masks, variance))
    return num_final / (1.0 + den_final)
```

```python
import functools

import jax
import jax.numpy as jnp
from jax import lax
from jax.experimental import pallas as pl
from jax.experimental.pallas import tpu as pltpu
from jax.sharding import PartitionSpec as P

MESH = pl.DeviceIdType.MESH
F32, BF16 = jnp.float32, jnp.bfloat16
TOP, BOT, KROWS = 128, 144, 160
HALO = 16
EXPS, ROWS, COLS, NB, KW = 2, 120, 1024, 9, 23
HALF = KW // 2
BLOCKS = 8
ORDERS = (0, 1, 1, 2, 2, 2, 3, 3, 3, 3)


def iota(shape, dim):
    return lax.broadcasted_iota(jnp.int32, shape, dim)


def kernel(
    n_sky, n_exp, coeffs, degrees, footprint, masks, taps, warped, variance, out,
    raw, halo, vraw, image, tapbuf, rowband, colband, gains, along, vsend, msend, vrecv, mrecv, weights,
    local_sems, halo_send, halo_recv, v_send, v_recv, m_send, m_recv,
):
    sky, me = lax.axis_index("sky"), lax.axis_index("exp")
    above, below = lax.rem(sky + n_sky - 1, n_sky), lax.rem(sky + 1, n_sky)
    peers = [lax.rem(me + t, n_exp) for t in range(n_exp)]

    own_copy = pltpu.make_async_copy(warped, raw, local_sems.at[0])
    var_copy = pltpu.make_async_copy(variance, vraw, local_sems.at[1])
    var_copy.start()
    own_copy.start()

    barrier = pltpu.get_barrier_semaphore()
    for t in range(1, n_exp):
        pl.semaphore_signal(barrier, inc=1, device_id=(sky, peers[t]), device_id_type=MESH)
    for row in (above, below):
        pl.semaphore_signal(barrier, inc=1, device_id=(row, me), device_id_type=MESH)

    tapbuf[...] = jnp.zeros_like(tapbuf)
    for b in range(NB):
        tapbuf[2 * b : 2 * b + 2, 0:KW] = taps[b].astype(F32)

    def band(row, k, valid):
        table = jnp.broadcast_to(tapbuf[row : row + 1, :], k.shape)
        picked = jnp.take_along_axis(table, jnp.clip(k, 0, 127), axis=1)
        return jnp.where(valid & (k >= 0) & (k < KW), picked, 0.0).astype(BF16)

    kappa, cols = iota((256, 128), 0), iota((256, 128), 1)
    k_col = kappa - cols - (64 - HALF)
    for b in range(NB):
        colband[b] = band(2 * b + 1, k_col, k_col == k_col)
    r_low, k_low = iota((128, 128), 0), iota((128, 128), 1)
    k_own = k_low - r_low + HALF
    valid_own = k_low < ROWS
    where_row = jnp.where(k_low < HALO, k_low - HALO, k_low + (ROWS - HALO))
    k_halo = where_row - r_low + HALF
    valid_halo = (k_low < 2 * HALO) & ((k_low >= HALO) | (sky > 0)) & ((k_low < HALO) | (sky < n_sky - 1))
    for b in range(NB):
        rowband[128 * b : 128 * b + 128, 0:128] = band(2 * b, k_own, valid_own)
        rowband[128 * b : 128 * b + 128, 128:KROWS] = band(2 * b, k_halo, valid_halo)[:, 0 : KROWS - 128]

    pl.semaphore_wait(barrier, n_exp - 1 + 2)

    down = pltpu.make_async_remote_copy(
        src_ref=warped.at[:, ROWS - HALO : ROWS, :], dst_ref=halo.at[0],
        send_sem=halo_send.at[0], recv_sem=halo_recv.at[0], device_id=(below, me), device_id_type=MESH,
    )
    up = pltpu.make_async_remote_copy(
        src_ref=warped.at[:, 0:HALO, :], dst_ref=halo.at[1],
        send_sem=halo_send.at[1], recv_sem=halo_recv.at[1], device_id=(above, me), device_id_type=MESH,
    )
    down.start()
    up.start()

    var_copy.wait()
    rows = iota((ROWS, 128), 0)
    word_at = (rows * 137) >> 11
    offset = 2 * (rows - 15 * word_at)
    for e in range(EXPS):
        word = jnp.zeros((ROWS, 128), jnp.int32)
        for i in range(ROWS // 15):
            word = jnp.where(word_at == i, masks[e, i], word)
        global_row = sky * ROWS + rows
        usable = (
            (((word >> offset) & 3) != 3)
            & (global_row >= footprint[e, 0])
            & (global_row < footprint[e, 1])
        )
        for t in range(n_exp):
            block = vraw[e, :, pl.ds(pl.multiple_of(peers[t] * 128, 128), 128)].astype(F32)
            masked = jnp.where(usable, block, 0.0).astype(BF16)
            if t == 0:
                vrecv[0, e] = masked
            else:
                vsend[t - 1, e] = masked

    v_copies, m_copies = [], []
    for t in range(1, n_exp):
        v_copies.append(pltpu.make_async_remote_copy(
            src_ref=vsend.at[t - 1], dst_ref=vrecv.at[t],
            send_sem=v_send.at[t], recv_sem=v_recv.at[t], device_id=(sky, peers[t]), device_id_type=MESH,
        ))
        m_copies.append(pltpu.make_async_remote_copy(
            src_ref=msend.at[t - 1], dst_ref=mrecv.at[t],
            send_sem=m_send.at[t], recv_sem=m_recv.at[t], device_id=(sky, peers[t]), device_id_type=MESH,
        ))
    for copy in v_copies:
        copy.start()

    u = (2.0 * (sky * ROWS + iota((128, 128), 0)).astype(F32) + 1.0) / (n_sky * ROWS) - 1.0

    @pl.loop(0, NB)
    def _(b):
        for e in range(EXPS):
            degree = degrees[e, b]
            c = [jnp.where(ORDERS[t] <= degree, coeffs[e, b, t], 0.0) for t in range(10)]
            span = slice(128 * e, 128 * e + 128)
            gains[b, 0, span, :] = ((c[6] * u + c[3]) * u + c[1]) * u + c[0]
            gains[b, 1, span, :] = (c[7] * u + c[4]) * u + c[2]
            gains[b, 2, span, :] = c[8] * u + c[5]

    own_copy.wait()
    for e in range(EXPS):
        image[e, :, 0:128] = jnp.zeros((KROWS, 128), BF16)
        image[e, :, 1024:1152] = jnp.zeros((KROWS, 128), BF16)
        image[e, 112:128, :] = jnp.zeros((16, 1152), BF16)
        image[e, 0:ROWS, 64:1088] = raw[e]
    down.wait_recv()
    up.wait_recv()
    for e in range(EXPS):
        image[e, TOP : TOP + HALO, 64:1088] = halo[0, e]
        image[e, BOT : BOT + HALO, 64:1088] = halo[1, e]

    for e in range(EXPS):
        @pl.loop(0, 9)
        def _(n):
            span = pl.ds(pl.multiple_of(n * 128, 128), 128)
            filtered = jnp.dot(rowband[...], image[e, :, span], preferred_element_type=F32).astype(BF16)
            for b in range(NB):
                along[b, 128 * e : 128 * e + 128, span] = filtered[128 * b : 128 * b + 128]

    def matched_block(j):
        col = pl.multiple_of(j * 128, 128)
        v = (2.0 * (j * 128 + iota((64, 128), 1)).astype(F32) + 1.0) / COLS - 1.0
        sums = [jnp.zeros((64, 128), F32) for _ in range(4)]
        for b in range(NB):
            filtered = jnp.dot(along[b, :, pl.ds(col, 256)], colband[b], preferred_element_type=F32)
            for part in range(4):
                e, span = part // 2, slice(64 * part, 64 * part + 64)
                cubic = jnp.where(degrees[e, b] >= 3, coeffs[e, b, 9], 0.0)
                field = ((cubic * v + gains[b, 2, span, :]) * v + gains[b, 1, span, :]) * v + gains[b, 0, span, :]
                sums[part] = sums[part] + field * filtered[span]
        return sums

    def put(ref, sums):
        for e in range(EXPS):
            ref[e, 0:64] = sums[2 * e].astype(BF16)
            ref[e, 64:ROWS] = sums[2 * e + 1][0 : ROWS - 64].astype(BF16)

    for t in range(1, n_exp):
        put(msend.at[t - 1], matched_block(peers[t]))
        m_copies[t - 1].start()
    put(mrecv.at[0], matched_block(peers[0]))

    halves = ((0, 64), (64, ROWS))
    den = [jnp.zeros((hi - lo, 128), F32) for lo, hi in halves]
    for t in range(n_exp):
        if t > 0:
            v_copies[t - 1].wait_recv()
        for i, (lo, hi) in enumerate(halves):
            for e in range(EXPS):
                var = vrecv[t, e, lo:hi].astype(F32)
                weight = jnp.where(var > 0.0, 1.0 / var, 0.0)
                weights[t, e, lo:hi] = weight
                den[i] = den[i] + weight
    num = [jnp.zeros((hi - lo, 128), F32) for lo, hi in halves]
    for t in range(n_exp):
        if t > 0:
            m_copies[t - 1].wait_recv()
        for i, (lo, hi) in enumerate(halves):
            for e in range(EXPS):
                num[i] = num[i] + weights[t, e, lo:hi] * mrecv[t, e, lo:hi].astype(F32)
    for i, (lo, hi) in enumerate(halves):
        first = num[i] / (1.0 + den[i])
        num_final = jnp.zeros((hi - lo, 128), F32)
        den_final = jnp.zeros((hi - lo, 128), F32)
        for t in range(n_exp):
            for e in range(EXPS):
                value = mrecv[t, e, lo:hi].astype(F32)
                weight = weights[t, e, lo:hi]
                excess = value - first
                robust = weight / (1.0 + excess * excess * weight * (1.0 / 9.0))
                num_final = num_final + robust * value
                den_final = den_final + robust
        out[lo:hi, :] = num_final / (1.0 + den_final)

    down.wait_send()
    up.wait_send()
    for copy in v_copies + m_copies:
        copy.wait_send()


def solution(mesh):
    n_sky, n_exp = mesh.shape["sky"], mesh.shape["exp"]

    def body(warped, variance, basis_taps, coeffs, degrees, footprint, masks):
        smem = pl.BlockSpec(memory_space=pltpu.SMEM)
        hbm = pl.BlockSpec(memory_space=pl.ANY)
        vmem = pl.BlockSpec(memory_space=pltpu.VMEM)
        dma = pltpu.SemaphoreType.DMA
        return pl.pallas_call(
            functools.partial(kernel, n_sky, n_exp),
            out_shape=jax.ShapeDtypeStruct((ROWS, 128), F32),
            in_specs=[smem, smem, smem, smem, vmem, hbm, hbm],
            out_specs=vmem,
            scratch_shapes=[
                pltpu.VMEM((EXPS, ROWS, COLS), BF16),
                pltpu.VMEM((2, EXPS, HALO, COLS), BF16),
                pltpu.VMEM((EXPS, ROWS, COLS), BF16),
                pltpu.VMEM((EXPS, KROWS, COLS + 128), BF16),
                pltpu.VMEM((24, 128), F32),
                pltpu.VMEM((NB * 128, KROWS), BF16),
                pltpu.VMEM((NB, 256, 128), BF16),
                pltpu.VMEM((NB, 3, 256, 128), F32),
                pltpu.VMEM((NB, 256, COLS + 128), BF16),
                pltpu.VMEM((n_exp - 1, EXPS, ROWS, 128), BF16),
                pltpu.VMEM((n_exp - 1, EXPS, ROWS, 128), BF16),
                pltpu.VMEM((n_exp, EXPS, ROWS, 128), BF16),
                pltpu.VMEM((n_exp, EXPS, ROWS, 128), BF16),
                pltpu.VMEM((n_exp, EXPS, ROWS, 128), F32),
                dma((2,)), dma((2,)), dma((2,)),
                dma((n_exp,)), dma((n_exp,)), dma((n_exp,)), dma((n_exp,)),
            ],
            compiler_params=pltpu.CompilerParams(
                collective_id=0, has_side_effects=True, vmem_limit_bytes=60 * 1024 * 1024
            ),
            name="coadd",
        )(coeffs, degrees, footprint, masks, basis_taps, warped, variance)

    in_specs = (
        P("exp", "sky", None),
        P("exp", "sky", None),
        P(),
        P("exp", None, None),
        P("exp", None),
        P("exp", None),
        P("exp", "sky"),
    )
    return jax.shard_map(body, mesh=mesh, in_specs=in_specs, out_specs=P("sky", "exp"), check_vma=False)
```

```python
import functools

import jax
import jax.numpy as jnp
from jax import lax
from jax.experimental import pallas as pl
from jax.experimental.pallas import tpu as pltpu
from jax.sharding import PartitionSpec as P

MESH = pl.DeviceIdType.MESH
F32, BF16 = jnp.float32, jnp.bfloat16
EXPS, ROWS, COLS, NB, KW = 2, 120, 1024, 9, 23
HALF = KW // 2
HALO = 16
TOP, BOT, KROWS = 128, 144, 160
PAD = 16
ORDERS = (0, 1, 1, 2, 2, 2, 3, 3, 3, 3)
STEP = 16.0 / COLS


def iota(shape, dim):
    return lax.broadcasted_iota(jnp.int32, shape, dim)


def kernel(
    n_sky, n_exp, coeffs_hbm, degrees_hbm, footprint_hbm, masks_hbm, taps_hbm, warped, variance, out,
    coeffs, degrees, footprint, masks, taps, raw, vraw, image, tapbuf, rowband, colband, gains, along,
    vsend, msend, vrecv, mrecv, weights,
    small_sems, local_sems, halo_send, halo_recv, v_send, v_recv, m_send, m_recv,
):
    sky, me = lax.axis_index("sky"), lax.axis_index("exp")
    not_first, not_last = sky > 0, sky < n_sky - 1
    peers = [lax.rem(me + t, n_exp) for t in range(n_exp)]

    barrier = pltpu.get_barrier_semaphore()

    @pl.when(not_last)
    def _():
        pl.semaphore_signal(barrier, inc=1, device_id=(sky + 1, me), device_id_type=MESH)

    @pl.when(not_first)
    def _():
        pl.semaphore_signal(barrier, inc=1, device_id=(sky - 1, me), device_id_type=MESH)

    for t in range(1, n_exp):
        pl.semaphore_signal(barrier, inc=1, device_id=(sky, peers[t]), device_id_type=MESH)

    small = [
        pltpu.make_async_copy(src, dst, small_sems.at[i])
        for i, (src, dst) in enumerate((
            (taps_hbm, taps), (masks_hbm, masks), (footprint_hbm, footprint), (coeffs_hbm, coeffs), (degrees_hbm, degrees),
        ))
    ]
    for copy in small:
        copy.start()
    var_copy = pltpu.make_async_copy(variance, vraw.at[:, 0:ROWS, :], local_sems.at[0])
    own_copy = pltpu.make_async_copy(warped, raw.at[:, 0:ROWS, :], local_sems.at[1])
    var_copy.start()
    own_copy.start()

    for e in range(EXPS):
        raw[e, ROWS:TOP, :] = jnp.zeros((TOP - ROWS, COLS), BF16)
        vraw[e, ROWS:128, :] = jnp.zeros((128 - ROWS, COLS), BF16)

    @pl.when(jnp.logical_not(not_first))
    def _():
        for e in range(EXPS):
            raw[e, TOP:BOT, :] = jnp.zeros((HALO, COLS), BF16)

    @pl.when(jnp.logical_not(not_last))
    def _():
        for e in range(EXPS):
            raw[e, BOT:KROWS, :] = jnp.zeros((HALO, COLS), BF16)

    tapbuf[...] = jnp.zeros_like(tapbuf)
    small[0].wait()
    for b in range(NB):
        tapbuf[2 * b : 2 * b + 2, 0:KW] = taps[b].astype(F32)

    def band(row, k, valid):
        table = jnp.broadcast_to(tapbuf[row : row + 1, :], k.shape)
        picked = jnp.take_along_axis(table, jnp.clip(k, 0, 127), axis=1)
        return jnp.where(valid & (k >= 0) & (k < KW), picked, 0.0).astype(BF16)

    low, lane = iota((128, 128), 0), iota((128, 128), 1)
    k_own = low - lane + HALF
    low_h, lane_h = iota((2 * HALO, 128), 0), iota((2 * HALO, 128), 1)
    k_halo = jnp.where(low_h < HALO, low_h - HALO, low_h + (ROWS - HALO)) - lane_h + HALF
    k_first = lane - low - (PAD - HALF)
    k_second = k_first + 128
    for b in range(NB):
        span = slice(128 * b, 128 * b + 128)
        rowband[0:TOP, span] = band(2 * b, k_own, low < ROWS)
        rowband[TOP:KROWS, span] = band(2 * b, k_halo, low_h >= 0)
        colband[b, :, 0:128] = band(2 * b + 1, k_first, low >= 0)
        colband[b, :, 128:KROWS] = band(2 * b + 1, k_second, low >= 0)[:, 0 : KROWS - 128]

    n_neighbours = not_first.astype(jnp.int32) + not_last.astype(jnp.int32)
    pl.semaphore_wait(barrier, n_exp - 1 + n_neighbours)

    down = pltpu.make_async_remote_copy(
        src_ref=warped.at[:, ROWS - HALO : ROWS, :], dst_ref=raw.at[:, TOP:BOT, :],
        send_sem=halo_send.at[0], recv_sem=halo_recv.at[0], device_id=(sky + 1, me), device_id_type=MESH,
    )
    up = pltpu.make_async_remote_copy(
        src_ref=warped.at[:, 0:HALO, :], dst_ref=raw.at[:, BOT:KROWS, :],
        send_sem=halo_send.at[1], recv_sem=halo_recv.at[1], device_id=(sky - 1, me), device_id_type=MESH,
    )

    @pl.when(not_last)
    def _():
        down.start()

    @pl.when(not_first)
    def _():
        up.start()

    small[1].wait()
    small[2].wait()
    var_copy.wait()
    rows = iota((8, 128), 1)
    word_at = (rows * 137) >> 11
    offset = 2 * (rows - 15 * word_at)
    for e in range(EXPS):
        word = jnp.zeros((8, 128), jnp.int32)
        for i in range(ROWS // 15):
            word = jnp.where(word_at == i, masks[e, i], word)
        global_row = sky * ROWS + rows
        usable = (
            (((word >> offset) & 3) != 3)
            & (global_row >= footprint[e, 0])
            & (global_row < footprint[e, 1])
            & (rows < ROWS)
        )
        keep = jnp.broadcast_to(usable.astype(F32)[0:1], (128, 128))
        for t in range(n_exp):
            block = vraw[e, :, pl.ds(pl.multiple_of(peers[t] * 128, 128), 128)].astype(F32).T
            masked = (block * keep).astype(BF16)
            if t == 0:
                vrecv[0, e] = masked
            else:
                vsend[t - 1, e] = masked

    v_copies, m_copies = [], []
    for t in range(1, n_exp):
        v_copies.append(pltpu.make_async_remote_copy(
            src_ref=vsend.at[t - 1], dst_ref=vrecv.at[t],
            send_sem=v_send.at[t], recv_sem=v_recv.at[t], device_id=(sky, peers[t]), device_id_type=MESH,
        ))
        m_copies.append(pltpu.make_async_remote_copy(
            src_ref=msend.at[t - 1], dst_ref=mrecv.at[t],
            send_sem=m_send.at[t], recv_sem=m_recv.at[t], device_id=(sky, peers[t]), device_id_type=MESH,
        ))
    for copy in v_copies:
        copy.start()

    small[3].wait()
    small[4].wait()
    u = (2.0 * (sky * ROWS + rows).astype(F32) + 1.0) / (n_sky * ROWS) - 1.0
    for b in range(NB):
        for e in range(EXPS):
            degree = degrees[e, b]
            c = [jnp.where(ORDERS[t] <= degree, coeffs[b, e, t], 0.0) for t in range(10)]
            gains[b, e, 0] = ((c[6] * u + c[3]) * u + c[1]) * u + c[0]
            gains[b, e, 1] = (c[7] * u + c[4]) * u + c[2]
            gains[b, e, 2] = c[8] * u + c[5]
            gains[b, e, 3] = jnp.full((8, 128), c[9], F32)

    for b in range(NB):
        along[b, 0:PAD, :] = jnp.zeros((PAD, 256), BF16)
        along[b, PAD + COLS : COLS + 2 * PAD, :] = jnp.zeros((PAD, 256), BF16)
    own_copy.wait()
    for e in range(EXPS):
        for i in range(COLS // 128):
            span = slice(128 * i, 128 * i + 128)
            image[e, span, 0:TOP] = raw[e, 0:TOP, span].astype(F32).T.astype(BF16)

    @pl.when(not_first)
    def _():
        down.wait_recv()

    @pl.when(not_last)
    def _():
        up.wait_recv()

    for e in range(EXPS):
        for i in range(COLS // 128):
            span = slice(128 * i, 128 * i + 128)
            image[e, span, TOP:KROWS] = raw[e, TOP:KROWS, span].astype(F32).T.astype(BF16)

    for e in range(EXPS):
        lanes = slice(128 * e, 128 * e + 128)

        @pl.loop(0, 4)
        def _(n):
            tile = rowband[:, pl.ds(pl.multiple_of(n * 256, 256), 256)]
            filtered = jnp.dot(image[e], tile, preferred_element_type=F32).astype(BF16)
            along[2 * n, PAD : PAD + COLS, lanes] = filtered[:, 0:128]
            along[2 * n + 1, PAD : PAD + COLS, lanes] = filtered[:, 128:256]

        filtered = jnp.dot(image[e], rowband[:, 1024:1152], preferred_element_type=F32).astype(BF16)
        along[8, PAD : PAD + COLS, lanes] = filtered

    def put_matched(ref, j):
        start = pl.multiple_of(j * 128, 128)
        v = (2.0 * (j * 128 + iota((8, 128), 0)).astype(F32) + 1.0) / COLS - 1.0
        first_arg = 2.0 * v + STEP
        second_arg = 3.0 * v * v + 3.0 * STEP * v + STEP * STEP
        third_arg = 3.0 * (v + STEP)
        sums = [[jnp.zeros((8, 128), F32) for _ in range(16)] for _ in range(EXPS)]
        for b in range(NB):
            window = along[b, pl.ds(start, KROWS), :]
            filtered = jnp.dot(colband[b], window, preferred_element_type=F32)
            for e in range(EXPS):
                g0, g1, g2, g3 = (gains[b, e, q] for q in range(4))
                field = ((g3 * v + g2) * v + g1) * v + g0
                d1 = (g1 + g2 * first_arg + g3 * second_arg) * STEP
                d2 = (g2 + g3 * third_arg) * (2.0 * STEP * STEP)
                d3 = g3 * (6.0 * STEP * STEP * STEP)
                for i in range(16):
                    part = filtered[8 * i : 8 * i + 8, 128 * e : 128 * e + 128]
                    sums[e][i] = sums[e][i] + field * part
                    if i < 15:
                        field = field + d1
                    if i < 14:
                        d1 = d1 + d2
                    if i < 13:
                        d2 = d2 + d3
        for e in range(EXPS):
            ref[e] = jnp.concatenate(sums[e], axis=0).astype(BF16)

    for t in range(1, n_exp):
        put_matched(msend.at[t - 1], peers[t])
        m_copies[t - 1].start()
    put_matched(mrecv.at[0], peers[0])

    halves = ((0, 64), (64, 128))
    zero = jnp.zeros((64, 128), F32)
    den = [zero, zero]
    for t in range(n_exp):
        if t > 0:
            v_copies[t - 1].wait_recv()
        for i, (lo, hi) in enumerate(halves):
            for e in range(EXPS):
                var = vrecv[t, e, lo:hi].astype(F32)
                weight = jnp.where(var > 0.0, 1.0 / var, 0.0)
                weights[t, e, lo:hi] = weight
                den[i] = den[i] + weight
    num = [zero, zero]
    for t in range(n_exp):
        if t > 0:
            m_copies[t - 1].wait_recv()
        for i, (lo, hi) in enumerate(halves):
            for e in range(EXPS):
                num[i] = num[i] + weights[t, e, lo:hi] * mrecv[t, e, lo:hi].astype(F32)
    finals = []
    for i, (lo, hi) in enumerate(halves):
        first = num[i] / (1.0 + den[i])
        num_final, den_final = zero, zero
        for t in range(n_exp):
            for e in range(EXPS):
                value = mrecv[t, e, lo:hi].astype(F32)
                weight = weights[t, e, lo:hi]
                excess = value - first
                robust = weight / (1.0 + excess * excess * weight * (1.0 / 9.0))
                num_final = num_final + robust * value
                den_final = den_final + robust
        finals.append(num_final / (1.0 + den_final))
    out[...] = jnp.concatenate(finals, axis=0).T[0:ROWS, :]

    @pl.when(not_last)
    def _():
        down.wait_send()

    @pl.when(not_first)
    def _():
        up.wait_send()

    for copy in v_copies + m_copies:
        copy.wait_send()


def solution(mesh):
    n_sky, n_exp = mesh.shape["sky"], mesh.shape["exp"]

    def body(warped, variance, basis_taps, coeffs, degrees, footprint, masks):
        hbm = pl.BlockSpec(memory_space=pl.ANY)
        vmem = pl.BlockSpec(memory_space=pltpu.VMEM)
        dma = pltpu.SemaphoreType.DMA
        return pl.pallas_call(
            functools.partial(kernel, n_sky, n_exp),
            out_shape=jax.ShapeDtypeStruct((ROWS, 128), F32),
            in_specs=[hbm] * 7,
            out_specs=vmem,
            scratch_shapes=[
                pltpu.SMEM((NB, EXPS, 10), F32),
                pltpu.SMEM((EXPS, NB), jnp.int32),
                pltpu.SMEM((EXPS, 2), jnp.int32),
                pltpu.SMEM((EXPS, 8), jnp.int32),
                pltpu.VMEM((NB, 2, KW), BF16),
                pltpu.VMEM((EXPS, KROWS, COLS), BF16),
                pltpu.VMEM((EXPS, 128, COLS), BF16),
                pltpu.VMEM((EXPS, COLS, KROWS), BF16),
                pltpu.VMEM((24, 128), F32),
                pltpu.VMEM((KROWS, NB * 128), BF16),
                pltpu.VMEM((NB, 128, KROWS), BF16),
                pltpu.VMEM((NB, EXPS, 4, 8, 128), F32),
                pltpu.VMEM((NB, COLS + 2 * PAD, 256), BF16),
                pltpu.VMEM((n_exp - 1, EXPS, 128, 128), BF16),
                pltpu.VMEM((n_exp - 1, EXPS, 128, 128), BF16),
                pltpu.VMEM((n_exp, EXPS, 128, 128), BF16),
                pltpu.VMEM((n_exp, EXPS, 128, 128), BF16),
                pltpu.VMEM((n_exp, EXPS, 128, 128), F32),
                dma((5,)), dma((2,)), dma((2,)), dma((2,)),
                dma((n_exp,)), dma((n_exp,)), dma((n_exp,)), dma((n_exp,)),
            ],
            compiler_params=pltpu.CompilerParams(
                collective_id=0, has_side_effects=True, vmem_limit_bytes=60 * 1024 * 1024
            ),
            name="coadd",
        )(coeffs.transpose(1, 0, 2), degrees, footprint, masks, basis_taps, warped, variance)

    in_specs = (
        P("exp", "sky", None),
        P("exp", "sky", None),
        P(),
        P("exp", None, None),
        P("exp", None),
        P("exp", None),
        P("exp", "sky"),
    )
    return jax.shard_map(body, mesh=mesh, in_specs=in_specs, out_specs=P("sky", "exp"), check_vma=False)
```

```python
import functools

import jax
import jax.numpy as jnp
from jax import lax
from jax.experimental import pallas as pl
from jax.experimental.pallas import tpu as pltpu
from jax.sharding import PartitionSpec as P

MESH = pl.DeviceIdType.MESH
F32, BF16 = jnp.float32, jnp.bfloat16
EXPS, ROWS, COLS, NB, KW = 2, 120, 1024, 9, 23
HALF = KW // 2
HALO = 16
LO, HI = 16, 104
INNER = HI - LO
EDGE = ROWS - INNER
EROWS = 96
PAD = 16
WINDOW = 160
ORDERS = (0, 1, 1, 2, 2, 2, 3, 3, 3, 3)
STEP = 16.0 / COLS


def iota(shape, dim):
    return lax.broadcasted_iota(jnp.int32, shape, dim)


def kernel(
    n_sky, n_exp, coeffs_hbm, degrees_hbm, footprint_hbm, masks_hbm, taps_hbm, warped, variance, out,
    coeffs, degrees, footprint, masks, taps, own, halo, vraw, image, edge_image, tapbuf, rowband, colband,
    edge_rowband, edge_colband, gains, edge_gains, along, edge_along,
    vsend, msend, esend, vrecv, mrecv, erecv, weights,
    small_sems, local_sems, halo_send, halo_recv, v_send, v_recv, m_send, m_recv, e_send, e_recv,
):
    sky, me = lax.axis_index("sky"), lax.axis_index("exp")
    not_first, not_last = sky > 0, sky < n_sky - 1
    peers = [lax.rem(me + t, n_exp) for t in range(n_exp)]

    barrier = pltpu.get_barrier_semaphore()

    @pl.when(not_last)
    def _():
        pl.semaphore_signal(barrier, inc=1, device_id=(sky + 1, me), device_id_type=MESH)

    @pl.when(not_first)
    def _():
        pl.semaphore_signal(barrier, inc=1, device_id=(sky - 1, me), device_id_type=MESH)

    for t in range(1, n_exp):
        pl.semaphore_signal(barrier, inc=1, device_id=(sky, peers[t]), device_id_type=MESH)

    small = [
        pltpu.make_async_copy(src, dst, small_sems.at[i])
        for i, (src, dst) in enumerate((
            (taps_hbm, taps), (masks_hbm, masks), (footprint_hbm, footprint), (coeffs_hbm, coeffs), (degrees_hbm, degrees),
        ))
    ]
    for copy in small:
        copy.start()
    var_copy = pltpu.make_async_copy(variance, vraw, local_sems.at[0])
    own_copy = pltpu.make_async_copy(warped, own, local_sems.at[1])
    var_copy.start()
    own_copy.start()

    @pl.when(jnp.logical_not(not_first))
    def _():
        halo[0] = jnp.zeros((EXPS, HALO, COLS), BF16)

    @pl.when(jnp.logical_not(not_last))
    def _():
        halo[1] = jnp.zeros((EXPS, HALO, COLS), BF16)

    tapbuf[...] = jnp.zeros_like(tapbuf)
    small[0].wait()
    for b in range(NB):
        tapbuf[2 * b : 2 * b + 2, 0:KW] = taps[b].astype(F32)

    def band(row, k):
        table = jnp.broadcast_to(tapbuf[row : row + 1, :], k.shape)
        picked = jnp.take_along_axis(table, jnp.clip(k, 0, 127), axis=1)
        return jnp.where((k >= 0) & (k < KW), picked, 0.0).astype(BF16)

    low, lane = iota((128, 128), 0), iota((128, 128), 1)
    k_row = jnp.where(low < ROWS, low - lane + HALF, -1)
    k_first = lane - low - (PAD - HALF)
    k_second = k_first + 128
    for b in range(NB):
        rowband[:, 128 * b : 128 * b + 128] = band(2 * b, k_row)
        colband[b, :, 0:128] = band(2 * b + 1, k_first)
        colband[b, :, 128:WINDOW] = band(2 * b + 1, k_second)[:, 0 : WINDOW - 128]

    small[1].wait()
    small[2].wait()
    var_copy.wait()
    rows = iota((ROWS, 128), 0)
    word_at = (rows * 137) >> 11
    offset = 2 * (rows - 15 * word_at)
    global_row = sky * ROWS + rows
    for e in range(EXPS):
        word = jnp.zeros((ROWS, 128), jnp.int32)
        for i in range(ROWS // 15):
            word = jnp.where(word_at == i, masks[e, i], word)
        usable = (
            (((word >> offset) & 3) != 3)
            & (global_row >= footprint[e, 0])
            & (global_row < footprint[e, 1])
        )
        for t in range(n_exp):
            block = vraw[e, :, pl.ds(pl.multiple_of(peers[t] * 128, 128), 128)].astype(F32)
            masked = jnp.where(usable, block, 0.0).astype(BF16)
            if t == 0:
                vrecv[0, e] = masked
            else:
                vsend[t - 1, e] = masked

    n_neighbours = not_first.astype(jnp.int32) + not_last.astype(jnp.int32)
    pl.semaphore_wait(barrier, n_exp - 1 + n_neighbours)

    down = pltpu.make_async_remote_copy(
        src_ref=warped.at[:, ROWS - HALO : ROWS, :], dst_ref=halo.at[0],
        send_sem=halo_send.at[0], recv_sem=halo_recv.at[0], device_id=(sky + 1, me), device_id_type=MESH,
    )
    up = pltpu.make_async_remote_copy(
        src_ref=warped.at[:, 0:HALO, :], dst_ref=halo.at[1],
        send_sem=halo_send.at[1], recv_sem=halo_recv.at[1], device_id=(sky - 1, me), device_id_type=MESH,
    )

    @pl.when(not_last)
    def _():
        down.start()

    @pl.when(not_first)
    def _():
        up.start()

    def to_peer(src, dst, send_sems, recv_sems, t):
        return pltpu.make_async_remote_copy(
            src_ref=src.at[t - 1], dst_ref=dst.at[t],
            send_sem=send_sems.at[t], recv_sem=recv_sems.at[t], device_id=(sky, peers[t]), device_id_type=MESH,
        )

    v_copies = [to_peer(vsend, vrecv, v_send, v_recv, t) for t in range(1, n_exp)]
    m_copies = [to_peer(msend, mrecv, m_send, m_recv, t) for t in range(1, n_exp)]
    e_copies = [to_peer(esend, erecv, e_send, e_recv, t) for t in range(1, n_exp)]
    for copy in v_copies:
        copy.start()

    small[3].wait()
    small[4].wait()

    def position(row):
        return (2.0 * (sky * ROWS + row).astype(F32) + 1.0) / (n_sky * ROWS) - 1.0

    def coefficients(b, e):
        degree = degrees[e, b]
        return [jnp.where(ORDERS[t] <= degree, coeffs[b, e, t], 0.0) for t in range(10)]

    def cubic(c, u):
        return ((c[6] * u + c[3]) * u + c[1]) * u + c[0], (c[7] * u + c[4]) * u + c[2], c[8] * u + c[5]

    u_lane = position(iota((8, 128), 1))
    i_edge = iota((EDGE, 128), 0)
    u_edge = position(jnp.where(i_edge < LO, i_edge, i_edge + INNER))
    for b in range(NB):
        for e in range(EXPS):
            c = coefficients(b, e)
            gains[b, e, 0], gains[b, e, 1], gains[b, e, 2] = cubic(c, u_lane)
            gains[b, e, 3] = jnp.full((8, 128), c[9], F32)

    for b in range(NB):
        along[b, 0:PAD, :] = jnp.zeros((PAD, 256), BF16)
        along[b, PAD + COLS : COLS + 2 * PAD, :] = jnp.zeros((PAD, 256), BF16)
    own_copy.wait()
    for e in range(EXPS):
        for i in range(COLS // 128):
            span = slice(128 * i, 128 * i + 128)
            block = jnp.concatenate([own[e, :, span].astype(F32), jnp.zeros((128 - ROWS, 128), F32)], axis=0)
            image[e, span, :] = block.T.astype(BF16)

    for e in range(EXPS):
        lanes = slice(128 * e, 128 * e + 128)

        @pl.loop(0, 4)
        def _(n):
            tile = rowband[:, pl.ds(pl.multiple_of(n * 256, 256), 256)]
            filtered = jnp.dot(image[e], tile, preferred_element_type=F32).astype(BF16)
            along[2 * n, PAD : PAD + COLS, lanes] = filtered[:, 0:128]
            along[2 * n + 1, PAD : PAD + COLS, lanes] = filtered[:, 128:256]

        filtered = jnp.dot(image[e], rowband[:, 1024:1152], preferred_element_type=F32).astype(BF16)
        along[8, PAD : PAD + COLS, lanes] = filtered

    def put_interior(ref, j):
        start = pl.multiple_of(j * 128, 128)
        v = (2.0 * (j * 128 + iota((8, 128), 0)).astype(F32) + 1.0) / COLS - 1.0
        first_arg = 2.0 * v + STEP
        second_arg = 3.0 * v * v + 3.0 * STEP * v + STEP * STEP
        third_arg = 3.0 * (v + STEP)
        sums = [[jnp.zeros((8, 128), F32) for _ in range(16)] for _ in range(EXPS)]
        for b in range(NB):
            window = along[b, pl.ds(start, WINDOW), :]
            filtered = jnp.dot(colband[b], window, preferred_element_type=F32)
            for e in range(EXPS):
                g0, g1, g2, g3 = (gains[b, e, q] for q in range(4))
                field = ((g3 * v + g2) * v + g1) * v + g0
                d1 = (g1 + g2 * first_arg + g3 * second_arg) * STEP
                d2 = (g2 + g3 * third_arg) * (2.0 * STEP * STEP)
                d3 = g3 * (6.0 * STEP * STEP * STEP)
                for i in range(16):
                    part = filtered[8 * i : 8 * i + 8, 128 * e : 128 * e + 128]
                    sums[e][i] = sums[e][i] + field * part
                    if i < 15:
                        field = field + d1
                    if i < 14:
                        d1 = d1 + d2
                    if i < 13:
                        d2 = d2 + d3
        for e in range(EXPS):
            ref[e] = jnp.concatenate(sums[e], axis=0).T[LO:HI].astype(BF16)

    for t in range(1, n_exp):
        put_interior(msend.at[t - 1], peers[t])
        m_copies[t - 1].start()
    put_interior(mrecv.at[0], peers[0])

    i_band, kappa = iota((EDGE, 128), 0), iota((EDGE, 128), 1)
    k_edge = (
        jnp.where(kappa < 48, kappa - HALO, kappa + 40) - jnp.where(i_band < LO, i_band, i_band + INNER) + HALF
    )
    k_edge = jnp.where(kappa < EROWS, k_edge, -1)
    kappa_col, col = iota((256, 128), 0), iota((256, 128), 1)
    k_edge_col = kappa_col - col - (64 - HALF)
    for b in range(NB):
        edge_rowband[EDGE * b : EDGE * b + EDGE, :] = band(2 * b, k_edge)[:, 0:EROWS]
        edge_colband[b] = band(2 * b + 1, k_edge_col)
        for e in range(EXPS):
            g = cubic(coefficients(b, e), u_edge)
            for q in range(3):
                edge_gains[b, q, EDGE * e : EDGE * e + EDGE, :] = g[q]
    for e in range(EXPS):
        edge_image[e, :, 0:128] = jnp.zeros((EROWS, 128), BF16)
        edge_image[e, :, 1024:1152] = jnp.zeros((EROWS, 128), BF16)
        edge_image[e, 16:48, 64:1088] = own[e, 0:32]
        edge_image[e, 48:80, 64:1088] = own[e, 88:120]

    @pl.when(not_first)
    def _():
        down.wait_recv()

    @pl.when(not_last)
    def _():
        up.wait_recv()

    for e in range(EXPS):
        edge_image[e, 0:16, 64:1088] = halo[0, e]
        edge_image[e, 80:96, 64:1088] = halo[1, e]

    for e in range(EXPS):
        for n in range(5):
            span = slice(256 * n, min(256 * n + 256, COLS + 128))
            filtered = jnp.dot(edge_rowband[...], edge_image[e, :, span], preferred_element_type=F32).astype(BF16)
            for b in range(NB):
                edge_along[b, EDGE * e : EDGE * e + EDGE, span] = filtered[EDGE * b : EDGE * b + EDGE]

    def put_edges(group):
        starts = [pl.multiple_of(peers[t] * 128, 128) for t in group]
        vs = [(2.0 * (peers[t] * 128 + iota((EDGE, 128), 1)).astype(F32) + 1.0) / COLS - 1.0 for t in group]
        sums = [[jnp.zeros((EDGE, 128), F32) for _ in range(EXPS)] for _ in group]
        for b in range(NB):
            windows = jnp.concatenate([edge_along[b, :, pl.ds(s, 256)] for s in starts], axis=0)
            filtered = jnp.dot(windows, edge_colband[b], preferred_element_type=F32)
            for e in range(EXPS):
                g3 = jnp.where(degrees[e, b] >= 3, coeffs[b, e, 9], 0.0)
                g0, g1, g2 = (edge_gains[b, q, EDGE * e : EDGE * e + EDGE, :] for q in range(3))
                for i, v in enumerate(vs):
                    part = filtered[2 * EDGE * i + EDGE * e : 2 * EDGE * i + EDGE * e + EDGE]
                    sums[i][e] = sums[i][e] + (((g3 * v + g2) * v + g1) * v + g0) * part
        for i, t in enumerate(group):
            ref = erecv.at[0] if t == 0 else esend.at[t - 1]
            for e in range(EXPS):
                ref[e] = sums[i][e].astype(BF16)
            if t > 0:
                e_copies[t - 1].start()

    put_edges((1, 2, 3, 4))
    put_edges((5, 6, 7, 0))

    inner_chunks = ((0, 48), (48, INNER))
    for t in range(n_exp):
        if t > 0:
            v_copies[t - 1].wait_recv()
        for e in range(EXPS):
            for lo, hi in ((0, LO), (LO, 64), (64, HI), (HI, ROWS)):
                var = vrecv[t, e, lo:hi].astype(F32)
                weights[t, e, lo:hi] = jnp.where(var > 0.0, 1.0 / var, 0.0)

    def coadd(values, weight_of, shape):
        num, den = jnp.zeros(shape, F32), jnp.zeros(shape, F32)
        for t in range(n_exp):
            for e in range(EXPS):
                weight = weight_of(t, e)
                num = num + weight * values(t, e)
                den = den + weight
        first = num / (1.0 + den)
        num, den = jnp.zeros(shape, F32), jnp.zeros(shape, F32)
        for t in range(n_exp):
            for e in range(EXPS):
                value, weight = values(t, e), weight_of(t, e)
                excess = value - first
                robust = weight / (1.0 + excess * excess * weight * (1.0 / 9.0))
                num = num + robust * value
                den = den + robust
        return num / (1.0 + den)

    for copy in m_copies:
        copy.wait_recv()
    for lo, hi in inner_chunks:
        out[LO + lo : LO + hi, :] = coadd(
            lambda t, e: mrecv[t, e, lo:hi].astype(F32), lambda t, e: weights[t, e, LO + lo : LO + hi], (hi - lo, 128)
        )
    for copy in e_copies:
        copy.wait_recv()
    edges = coadd(
        lambda t, e: erecv[t, e].astype(F32),
        lambda t, e: jnp.concatenate([weights[t, e, 0:LO], weights[t, e, HI:ROWS]], axis=0),
        (EDGE, 128),
    )
    out[0:LO, :] = edges[0:LO]
    out[HI:ROWS, :] = edges[LO:EDGE]

    @pl.when(not_last)
    def _():
        down.wait_send()

    @pl.when(not_first)
    def _():
        up.wait_send()

    for copy in v_copies + m_copies + e_copies:
        copy.wait_send()


def solution(mesh):
    n_sky, n_exp = mesh.shape["sky"], mesh.shape["exp"]

    def body(warped, variance, basis_taps, coeffs, degrees, footprint, masks):
        hbm = pl.BlockSpec(memory_space=pl.ANY)
        vmem = pl.BlockSpec(memory_space=pltpu.VMEM)
        dma = pltpu.SemaphoreType.DMA
        return pl.pallas_call(
            functools.partial(kernel, n_sky, n_exp),
            out_shape=jax.ShapeDtypeStruct((ROWS, 128), F32),
            in_specs=[hbm] * 7,
            out_specs=vmem,
            scratch_shapes=[
                pltpu.SMEM((NB, EXPS, 10), F32),
                pltpu.SMEM((EXPS, NB), jnp.int32),
                pltpu.SMEM((EXPS, 2), jnp.int32),
                pltpu.SMEM((EXPS, 8), jnp.int32),
                pltpu.VMEM((NB, 2, KW), BF16),
                pltpu.VMEM((EXPS, ROWS, COLS), BF16),
                pltpu.VMEM((2, EXPS, HALO, COLS), BF16),
                pltpu.VMEM((EXPS, ROWS, COLS), BF16),
                pltpu.VMEM((EXPS, COLS, 128), BF16),
                pltpu.VMEM((EXPS, EROWS, COLS + 128), BF16),
                pltpu.VMEM((24, 128), F32),
                pltpu.VMEM((128, NB * 128), BF16),
                pltpu.VMEM((NB, 128, WINDOW), BF16),
                pltpu.VMEM((NB * EDGE, EROWS), BF16),
                pltpu.VMEM((NB, 256, 128), BF16),
                pltpu.VMEM((NB, EXPS, 4, 8, 128), F32),
                pltpu.VMEM((NB, 3, EXPS * EDGE, 128), F32),
                pltpu.VMEM((NB, COLS + 2 * PAD, 256), BF16),
                pltpu.VMEM((NB, EXPS * EDGE, COLS + 128), BF16),
                pltpu.VMEM((n_exp - 1, EXPS, ROWS, 128), BF16),
                pltpu.VMEM((n_exp - 1, EXPS, INNER, 128), BF16),
                pltpu.VMEM((n_exp - 1, EXPS, EDGE, 128), BF16),
                pltpu.VMEM((n_exp, EXPS, ROWS, 128), BF16),
                pltpu.VMEM((n_exp, EXPS, INNER, 128), BF16),
                pltpu.VMEM((n_exp, EXPS, EDGE, 128), BF16),
                pltpu.VMEM((n_exp, EXPS, ROWS, 128), F32),
                dma((5,)), dma((2,)), dma((2,)), dma((2,)),
                dma((n_exp,)), dma((n_exp,)), dma((n_exp,)), dma((n_exp,)), dma((n_exp,)), dma((n_exp,)),
            ],
            compiler_params=pltpu.CompilerParams(
                collective_id=0, has_side_effects=True, vmem_limit_bytes=60 * 1024 * 1024
            ),
            name="coadd",
        )(coeffs.transpose(1, 0, 2), degrees, footprint, masks, basis_taps, warped, variance)

    in_specs = (
        P("exp", "sky", None),
        P("exp", "sky", None),
        P(),
        P("exp", None, None),
        P("exp", None),
        P("exp", None),
        P("exp", "sky"),
    )
    return jax.shard_map(body, mesh=mesh, in_specs=in_specs, out_specs=P("sky", "exp"), check_vma=False)
```

```python
import functools

import jax
import jax.numpy as jnp
from jax import lax
from jax.experimental import pallas as pl
from jax.experimental.pallas import tpu as pltpu
from jax.sharding import PartitionSpec as P

MESH = pl.DeviceIdType.MESH
F32, BF16 = jnp.float32, jnp.bfloat16
EXPS, ROWS, COLS, NB, KW = 2, 120, 1024, 9, 23
HALF = KW // 2
HALO = 16
LO, HI = 16, 104
INNER = HI - LO
EDGE = ROWS - INNER
EROWS = 96
PAD = 16
WINDOW = 160
ORDERS = (0, 1, 1, 2, 2, 2, 3, 3, 3, 3)
STEP = 16.0 / COLS
RING = 4
OFFSETS = ((0, 0), (2, 1), (2, 0), (1, 1), (3, 1), (0, 1), (1, 0), (3, 0))


def iota(shape, dim):
    return lax.broadcasted_iota(jnp.int32, shape, dim)


def kernel(
    n_sky, n_exp, coeffs_hbm, degrees_hbm, footprint_hbm, masks_hbm, taps_hbm, warped, variance, out,
    coeffs, degrees, footprint, masks, taps, own, halo, vraw, image, edge_image, tapbuf, rowband, colband,
    edge_rowband, edge_colband, gains, edge_gains, along, edge_along,
    vsend, msend, esend, vrecv, mrecv, erecv, weights,
    small_sems, local_sems, halo_send, halo_recv, v_send, v_recv, m_send, m_recv, e_send, e_recv,
):
    sky, me = lax.axis_index("sky"), lax.axis_index("exp")
    not_first, not_last = sky > 0, sky < n_sky - 1
    ring, pair = lax.rem(me, RING), me // RING
    peers = [lax.rem(pair + dz, n_exp // RING) * RING + lax.rem(ring + dx, RING) for dx, dz in OFFSETS]

    barrier = pltpu.get_barrier_semaphore()

    @pl.when(not_last)
    def _():
        pl.semaphore_signal(barrier, inc=1, device_id=(sky + 1, me), device_id_type=MESH)

    @pl.when(not_first)
    def _():
        pl.semaphore_signal(barrier, inc=1, device_id=(sky - 1, me), device_id_type=MESH)

    for t in range(1, n_exp):
        pl.semaphore_signal(barrier, inc=1, device_id=(sky, peers[t]), device_id_type=MESH)

    small = [
        pltpu.make_async_copy(src, dst, small_sems.at[i])
        for i, (src, dst) in enumerate((
            (taps_hbm, taps), (masks_hbm, masks), (footprint_hbm, footprint), (coeffs_hbm, coeffs), (degrees_hbm, degrees),
        ))
    ]
    for copy in small:
        copy.start()
    var_copy = pltpu.make_async_copy(variance, vraw, local_sems.at[0])
    own_copy = pltpu.make_async_copy(warped, own, local_sems.at[1])
    var_copy.start()
    own_copy.start()

    @pl.when(jnp.logical_not(not_first))
    def _():
        halo[0] = jnp.zeros((EXPS, HALO, COLS), BF16)

    @pl.when(jnp.logical_not(not_last))
    def _():
        halo[1] = jnp.zeros((EXPS, HALO, COLS), BF16)

    tapbuf[...] = jnp.zeros_like(tapbuf)
    small[0].wait()
    for b in range(NB):
        tapbuf[2 * b : 2 * b + 2, 0:KW] = taps[b].astype(F32)

    def band(row, k):
        table = jnp.broadcast_to(tapbuf[row : row + 1, :], k.shape)
        picked = jnp.take_along_axis(table, jnp.clip(k, 0, 127), axis=1)
        return jnp.where((k >= 0) & (k < KW), picked, 0.0).astype(BF16)

    low, lane = iota((128, 128), 0), iota((128, 128), 1)
    k_row = jnp.where(low < ROWS, low - lane + HALF, -1)
    k_first = lane - low - (PAD - HALF)
    k_second = k_first + 128
    for b in range(NB):
        rowband[:, 128 * b : 128 * b + 128] = band(2 * b, k_row)
        colband[b, :, 0:128] = band(2 * b + 1, k_first)
        colband[b, :, 128:WINDOW] = band(2 * b + 1, k_second)[:, 0 : WINDOW - 128]

    small[1].wait()
    small[2].wait()
    var_copy.wait()
    rows = iota((ROWS, 128), 0)
    word_at = (rows * 137) >> 11
    offset = 2 * (rows - 15 * word_at)
    global_row = sky * ROWS + rows
    for e in range(EXPS):
        word = jnp.zeros((ROWS, 128), jnp.int32)
        for i in range(ROWS // 15):
            word = jnp.where(word_at == i, masks[e, i], word)
        usable = (
            (((word >> offset) & 3) != 3)
            & (global_row >= footprint[e, 0])
            & (global_row < footprint[e, 1])
        )
        for t in range(n_exp):
            block = vraw[e, :, pl.ds(pl.multiple_of(peers[t] * 128, 128), 128)].astype(F32)
            masked = jnp.where(usable, block, 0.0).astype(BF16)
            if t == 0:
                vrecv[0, e] = masked
            else:
                vsend[t - 1, e] = masked

    n_neighbours = not_first.astype(jnp.int32) + not_last.astype(jnp.int32)
    pl.semaphore_wait(barrier, n_exp - 1 + n_neighbours)

    down = pltpu.make_async_remote_copy(
        src_ref=warped.at[:, ROWS - HALO : ROWS, :], dst_ref=halo.at[0],
        send_sem=halo_send.at[0], recv_sem=halo_recv.at[0], device_id=(sky + 1, me), device_id_type=MESH,
    )
    up = pltpu.make_async_remote_copy(
        src_ref=warped.at[:, 0:HALO, :], dst_ref=halo.at[1],
        send_sem=halo_send.at[1], recv_sem=halo_recv.at[1], device_id=(sky - 1, me), device_id_type=MESH,
    )

    @pl.when(not_last)
    def _():
        down.start()

    @pl.when(not_first)
    def _():
        up.start()

    def to_peer(src, dst, send_sems, recv_sems, t):
        return pltpu.make_async_remote_copy(
            src_ref=src.at[t - 1], dst_ref=dst.at[t],
            send_sem=send_sems.at[t], recv_sem=recv_sems.at[t], device_id=(sky, peers[t]), device_id_type=MESH,
        )

    v_copies = [to_peer(vsend, vrecv, v_send, v_recv, t) for t in range(1, n_exp)]
    m_copies = [to_peer(msend, mrecv, m_send, m_recv, t) for t in range(1, n_exp)]
    e_copies = [to_peer(esend, erecv, e_send, e_recv, t) for t in range(1, n_exp)]
    for copy in v_copies:
        copy.start()

    small[3].wait()
    small[4].wait()

    def position(row):
        return (2.0 * (sky * ROWS + row).astype(F32) + 1.0) / (n_sky * ROWS) - 1.0

    def coefficients(b, e):
        degree = degrees[e, b]
        return [jnp.where(ORDERS[t] <= degree, coeffs[b, e, t], 0.0) for t in range(10)]

    def cubic(c, u):
        return ((c[6] * u + c[3]) * u + c[1]) * u + c[0], (c[7] * u + c[4]) * u + c[2], c[8] * u + c[5]

    u_lane = position(iota((8, 128), 1))
    i_edge = iota((EDGE, 128), 0)
    u_edge = position(jnp.where(i_edge < LO, i_edge, i_edge + INNER))
    for b in range(NB):
        for e in range(EXPS):
            c = coefficients(b, e)
            gains[b, e, 0], gains[b, e, 1], gains[b, e, 2] = cubic(c, u_lane)
            gains[b, e, 3] = jnp.full((8, 128), c[9], F32)

    for b in range(NB):
        along[b, 0:PAD, :] = jnp.zeros((PAD, 256), BF16)
        along[b, PAD + COLS : COLS + 2 * PAD, :] = jnp.zeros((PAD, 256), BF16)
    own_copy.wait()
    for e in range(EXPS):
        for i in range(COLS // 128):
            span = slice(128 * i, 128 * i + 128)
            block = jnp.concatenate([own[e, :, span].astype(F32), jnp.zeros((128 - ROWS, 128), F32)], axis=0)
            image[e, span, :] = block.T.astype(BF16)

    for e in range(EXPS):
        lanes = slice(128 * e, 128 * e + 128)

        @pl.loop(0, 4)
        def _(n):
            tile = rowband[:, pl.ds(pl.multiple_of(n * 256, 256), 256)]
            filtered = jnp.dot(image[e], tile, preferred_element_type=F32).astype(BF16)
            along[2 * n, PAD : PAD + COLS, lanes] = filtered[:, 0:128]
            along[2 * n + 1, PAD : PAD + COLS, lanes] = filtered[:, 128:256]

        filtered = jnp.dot(image[e], rowband[:, 1024:1152], preferred_element_type=F32).astype(BF16)
        along[8, PAD : PAD + COLS, lanes] = filtered

    def put_interior(ref, j):
        start = pl.multiple_of(j * 128, 128)
        v = (2.0 * (j * 128 + iota((8, 128), 0)).astype(F32) + 1.0) / COLS - 1.0
        first_arg = 2.0 * v + STEP
        second_arg = 3.0 * v * v + 3.0 * STEP * v + STEP * STEP
        third_arg = 3.0 * (v + STEP)
        sums = [[jnp.zeros((8, 128), F32) for _ in range(16)] for _ in range(EXPS)]
        for b in range(NB):
            window = along[b, pl.ds(start, WINDOW), :]
            filtered = jnp.dot(colband[b], window, preferred_element_type=F32)
            for e in range(EXPS):
                g0, g1, g2, g3 = (gains[b, e, q] for q in range(4))
                field = ((g3 * v + g2) * v + g1) * v + g0
                d1 = (g1 + g2 * first_arg + g3 * second_arg) * STEP
                d2 = (g2 + g3 * third_arg) * (2.0 * STEP * STEP)
                d3 = g3 * (6.0 * STEP * STEP * STEP)
                for i in range(16):
                    part = filtered[8 * i : 8 * i + 8, 128 * e : 128 * e + 128]
                    sums[e][i] = sums[e][i] + field * part
                    if i < 15:
                        field = field + d1
                    if i < 14:
                        d1 = d1 + d2
                    if i < 13:
                        d2 = d2 + d3
        for e in range(EXPS):
            ref[e] = jnp.concatenate(sums[e], axis=0).T[LO:HI].astype(BF16)

    for t in range(1, n_exp):
        put_interior(msend.at[t - 1], peers[t])
        m_copies[t - 1].start()
    put_interior(mrecv.at[0], peers[0])

    i_band, kappa = iota((EDGE, 128), 0), iota((EDGE, 128), 1)
    k_edge = (
        jnp.where(kappa < 48, kappa - HALO, kappa + 40) - jnp.where(i_band < LO, i_band, i_band + INNER) + HALF
    )
    k_edge = jnp.where(kappa < EROWS, k_edge, -1)
    kappa_col, col = iota((256, 128), 0), iota((256, 128), 1)
    k_edge_col = kappa_col - col - (64 - HALF)
    for b in range(NB):
        edge_rowband[EDGE * b : EDGE * b + EDGE, :] = band(2 * b, k_edge)[:, 0:EROWS]
        edge_colband[b] = band(2 * b + 1, k_edge_col)
        for e in range(EXPS):
            g = cubic(coefficients(b, e), u_edge)
            for q in range(3):
                edge_gains[b, q, EDGE * e : EDGE * e + EDGE, :] = g[q]
    for e in range(EXPS):
        edge_image[e, :, 0:128] = jnp.zeros((EROWS, 128), BF16)
        edge_image[e, :, 1024:1152] = jnp.zeros((EROWS, 128), BF16)
        edge_image[e, 16:48, 64:1088] = own[e, 0:32]
        edge_image[e, 48:80, 64:1088] = own[e, 88:120]

    @pl.when(not_first)
    def _():
        down.wait_recv()

    @pl.when(not_last)
    def _():
        up.wait_recv()

    for e in range(EXPS):
        edge_image[e, 0:16, 64:1088] = halo[0, e]
        edge_image[e, 80:96, 64:1088] = halo[1, e]

    for e in range(EXPS):
        for n in range(5):
            span = slice(256 * n, min(256 * n + 256, COLS + 128))
            filtered = jnp.dot(edge_rowband[...], edge_image[e, :, span], preferred_element_type=F32).astype(BF16)
            for b in range(NB):
                edge_along[b, EDGE * e : EDGE * e + EDGE, span] = filtered[EDGE * b : EDGE * b + EDGE]

    def put_edges(group):
        starts = [pl.multiple_of(peers[t] * 128, 128) for t in group]
        vs = [(2.0 * (peers[t] * 128 + iota((EDGE, 128), 1)).astype(F32) + 1.0) / COLS - 1.0 for t in group]
        sums = [[jnp.zeros((EDGE, 128), F32) for _ in range(EXPS)] for _ in group]
        for b in range(NB):
            windows = jnp.concatenate([edge_along[b, :, pl.ds(s, 256)] for s in starts], axis=0)
            filtered = jnp.dot(windows, edge_colband[b], preferred_element_type=F32)
            for e in range(EXPS):
                g3 = jnp.where(degrees[e, b] >= 3, coeffs[b, e, 9], 0.0)
                g0, g1, g2 = (edge_gains[b, q, EDGE * e : EDGE * e + EDGE, :] for q in range(3))
                for i, v in enumerate(vs):
                    part = filtered[2 * EDGE * i + EDGE * e : 2 * EDGE * i + EDGE * e + EDGE]
                    sums[i][e] = sums[i][e] + (((g3 * v + g2) * v + g1) * v + g0) * part
        for i, t in enumerate(group):
            ref = erecv.at[0] if t == 0 else esend.at[t - 1]
            for e in range(EXPS):
                ref[e] = sums[i][e].astype(BF16)
            if t > 0:
                e_copies[t - 1].start()

    put_edges((1, 2, 3, 4))
    put_edges((5, 6, 7, 0))

    inner_chunks = ((0, 48), (48, INNER))
    for t in range(n_exp):
        if t > 0:
            v_copies[t - 1].wait_recv()
        for e in range(EXPS):
            for lo, hi in ((0, LO), (LO, 64), (64, HI), (HI, ROWS)):
                var = vrecv[t, e, lo:hi].astype(F32)
                weights[t, e, lo:hi] = jnp.where(var > 0.0, 1.0 / var, 0.0)

    def coadd(values, weight_of, shape):
        num, den = jnp.zeros(shape, F32), jnp.zeros(shape, F32)
        for t in range(n_exp):
            for e in range(EXPS):
                weight = weight_of(t, e)
                num = num + weight * values(t, e)
                den = den + weight
        first = num / (1.0 + den)
        num, den = jnp.zeros(shape, F32), jnp.zeros(shape, F32)
        for t in range(n_exp):
            for e in range(EXPS):
                value, weight = values(t, e), weight_of(t, e)
                excess = value - first
                robust = weight / (1.0 + excess * excess * weight * (1.0 / 9.0))
                num = num + robust * value
                den = den + robust
        return num / (1.0 + den)

    for copy in m_copies:
        copy.wait_recv()
    for lo, hi in inner_chunks:
        out[LO + lo : LO + hi, :] = coadd(
            lambda t, e: mrecv[t, e, lo:hi].astype(F32), lambda t, e: weights[t, e, LO + lo : LO + hi], (hi - lo, 128)
        )
    for copy in e_copies:
        copy.wait_recv()
    edges = coadd(
        lambda t, e: erecv[t, e].astype(F32),
        lambda t, e: jnp.concatenate([weights[t, e, 0:LO], weights[t, e, HI:ROWS]], axis=0),
        (EDGE, 128),
    )
    out[0:LO, :] = edges[0:LO]
    out[HI:ROWS, :] = edges[LO:EDGE]

    @pl.when(not_last)
    def _():
        down.wait_send()

    @pl.when(not_first)
    def _():
        up.wait_send()

    for copy in v_copies + m_copies + e_copies:
        copy.wait_send()


def solution(mesh):
    n_sky, n_exp = mesh.shape["sky"], mesh.shape["exp"]

    def body(warped, variance, basis_taps, coeffs, degrees, footprint, masks):
        hbm = pl.BlockSpec(memory_space=pl.ANY)
        vmem = pl.BlockSpec(memory_space=pltpu.VMEM)
        dma = pltpu.SemaphoreType.DMA
        return pl.pallas_call(
            functools.partial(kernel, n_sky, n_exp),
            out_shape=pltpu.VMEM((ROWS, 128), F32),
            in_specs=[hbm] * 7,
            out_specs=vmem,
            scratch_shapes=[
                pltpu.SMEM((NB, EXPS, 10), F32),
                pltpu.SMEM((EXPS, NB), jnp.int32),
                pltpu.SMEM((EXPS, 2), jnp.int32),
                pltpu.SMEM((EXPS, 8), jnp.int32),
                pltpu.VMEM((NB, 2, KW), BF16),
                pltpu.VMEM((EXPS, ROWS, COLS), BF16),
                pltpu.VMEM((2, EXPS, HALO, COLS), BF16),
                pltpu.VMEM((EXPS, ROWS, COLS), BF16),
                pltpu.VMEM((EXPS, COLS, 128), BF16),
                pltpu.VMEM((EXPS, EROWS, COLS + 128), BF16),
                pltpu.VMEM((24, 128), F32),
                pltpu.VMEM((128, NB * 128), BF16),
                pltpu.VMEM((NB, 128, WINDOW), BF16),
                pltpu.VMEM((NB * EDGE, EROWS), BF16),
                pltpu.VMEM((NB, 256, 128), BF16),
                pltpu.VMEM((NB, EXPS, 4, 8, 128), F32),
                pltpu.VMEM((NB, 3, EXPS * EDGE, 128), F32),
                pltpu.VMEM((NB, COLS + 2 * PAD, 256), BF16),
                pltpu.VMEM((NB, EXPS * EDGE, COLS + 128), BF16),
                pltpu.VMEM((n_exp - 1, EXPS, ROWS, 128), BF16),
                pltpu.VMEM((n_exp - 1, EXPS, INNER, 128), BF16),
                pltpu.VMEM((n_exp - 1, EXPS, EDGE, 128), BF16),
                pltpu.VMEM((n_exp, EXPS, ROWS, 128), BF16),
                pltpu.VMEM((n_exp, EXPS, INNER, 128), BF16),
                pltpu.VMEM((n_exp, EXPS, EDGE, 128), BF16),
                pltpu.VMEM((n_exp, EXPS, ROWS, 128), F32),
                dma((5,)), dma((2,)), dma((2,)), dma((2,)),
                dma((n_exp,)), dma((n_exp,)), dma((n_exp,)), dma((n_exp,)), dma((n_exp,)), dma((n_exp,)),
            ],
            compiler_params=pltpu.CompilerParams(
                collective_id=0, has_side_effects=True, vmem_limit_bytes=60 * 1024 * 1024
            ),
            name="coadd",
        )(coeffs.transpose(1, 0, 2), degrees, footprint, masks, basis_taps, warped, variance)

    in_specs = (
        P("exp", "sky", None),
        P("exp", "sky", None),
        P(),
        P("exp", None, None),
        P("exp", None),
        P("exp", None),
        P("exp", "sky"),
    )
    return jax.shard_map(body, mesh=mesh, in_specs=in_specs, out_specs=P("sky", "exp"), check_vma=False)
```

```python
import functools

import jax
import jax.numpy as jnp
from jax import lax
from jax.experimental import pallas as pl
from jax.experimental.pallas import tpu as pltpu
from jax.sharding import PartitionSpec as P

MESH = pl.DeviceIdType.MESH
F32, BF16 = jnp.float32, jnp.bfloat16
EXPS, ROWS, COLS, NB, KW = 2, 120, 1024, 9, 23
HALF = KW // 2
HALO = 16
LO, HI = 16, 104
INNER = HI - LO
EDGE = ROWS - INNER
EROWS = 96
PAD = 16
WINDOW = 160
ORDERS = (0, 1, 1, 2, 2, 2, 3, 3, 3, 3)
STEP = 16.0 / COLS
RING = 4
OFFSETS = ((0, 0), (2, 1), (2, 0), (1, 1), (3, 1), (0, 1), (1, 0), (3, 0))


def iota(shape, dim):
    return lax.broadcasted_iota(jnp.int32, shape, dim)


def kernel(
    n_sky, n_exp, coeffs_hbm, degrees_hbm, footprint_hbm, masks_hbm, taps_hbm, warped, variance, out,
    coeffs, degrees, footprint, masks, taps, own, halo, vraw, image, edge_image, tapbuf, rowband, colband,
    edge_rowband, edge_colband, gains, edge_gains, along, edge_along,
    vsend, msend, esend, vrecv, mrecv, erecv, weights,
    small_sems, local_sems, halo_send, halo_recv, v_send, v_recv, m_send, m_recv, e_send, e_recv,
):
    sky, me = lax.axis_index("sky"), lax.axis_index("exp")
    not_first, not_last = sky > 0, sky < n_sky - 1
    ring, pair = lax.rem(me, RING), me // RING
    peers = [lax.rem(pair + dz, n_exp // RING) * RING + lax.rem(ring + dx, RING) for dx, dz in OFFSETS]

    barrier = pltpu.get_barrier_semaphore()

    @pl.when(not_last)
    def _():
        pl.semaphore_signal(barrier, inc=1, device_id=(sky + 1, me), device_id_type=MESH)

    @pl.when(not_first)
    def _():
        pl.semaphore_signal(barrier, inc=1, device_id=(sky - 1, me), device_id_type=MESH)

    for t in range(1, n_exp):
        pl.semaphore_signal(barrier, inc=1, device_id=(sky, peers[t]), device_id_type=MESH)

    small = [
        pltpu.make_async_copy(src, dst, small_sems.at[i])
        for i, (src, dst) in enumerate((
            (taps_hbm, taps), (masks_hbm, masks), (footprint_hbm, footprint), (coeffs_hbm, coeffs), (degrees_hbm, degrees),
        ))
    ]
    for copy in small:
        copy.start()
    var_copy = pltpu.make_async_copy(variance, vraw, local_sems.at[0])
    own_copy = pltpu.make_async_copy(warped, own, local_sems.at[1])
    var_copy.start()
    own_copy.start()

    @pl.when(jnp.logical_not(not_first))
    def _():
        halo[0] = jnp.zeros((EXPS, HALO, COLS), BF16)

    @pl.when(jnp.logical_not(not_last))
    def _():
        halo[1] = jnp.zeros((EXPS, HALO, COLS), BF16)

    tapbuf[...] = jnp.zeros_like(tapbuf)
    small[0].wait()
    for b in range(NB):
        tapbuf[2 * b : 2 * b + 2, 0:KW] = taps[b].astype(F32)

    def band(row, k):
        table = jnp.broadcast_to(tapbuf[row : row + 1, :], k.shape)
        picked = jnp.take_along_axis(table, jnp.clip(k, 0, 127), axis=1)
        return jnp.where((k >= 0) & (k < KW), picked, 0.0).astype(BF16)

    low, lane = iota((128, 128), 0), iota((128, 128), 1)
    k_row = jnp.where(low < ROWS, low - lane + HALF, -1)
    k_first = lane - low - (PAD - HALF)
    k_second = k_first + 128
    tail = 96
    for b in range(NB):
        rowband[:, 128 * b : 128 * b + 128] = band(2 * b, k_row)
        colband[b, :, 0:128] = band(2 * b + 1, k_first)
        colband[b, 0:tail, 128:WINDOW] = jnp.zeros((tail, WINDOW - 128), BF16)
        colband[b, tail:128, 128:WINDOW] = band(2 * b + 1, k_second[tail:128])[:, 0 : WINDOW - 128]

    small[1].wait()
    small[2].wait()
    var_copy.wait()
    rows = iota((ROWS, 128), 0)
    word_at = (rows * 137) >> 11
    offset = 2 * (rows - 15 * word_at)
    global_row = sky * ROWS + rows
    for e in range(EXPS):
        word = jnp.zeros((ROWS, 128), jnp.int32)
        for i in range(ROWS // 15):
            word = jnp.where(word_at == i, masks[e, i], word)
        usable = (
            (((word >> offset) & 3) != 3)
            & (global_row >= footprint[e, 0])
            & (global_row < footprint[e, 1])
        )
        for t in range(n_exp):
            block = vraw[e, :, pl.ds(pl.multiple_of(peers[t] * 128, 128), 128)].astype(F32)
            masked = jnp.where(usable, block, 0.0).astype(BF16)
            if t == 0:
                vrecv[0, e] = masked
            else:
                vsend[t - 1, e] = masked

    n_neighbours = not_first.astype(jnp.int32) + not_last.astype(jnp.int32)
    pl.semaphore_wait(barrier, n_exp - 1 + n_neighbours)

    down = pltpu.make_async_remote_copy(
        src_ref=warped.at[:, ROWS - HALO : ROWS, :], dst_ref=halo.at[0],
        send_sem=halo_send.at[0], recv_sem=halo_recv.at[0], device_id=(sky + 1, me), device_id_type=MESH,
    )
    up = pltpu.make_async_remote_copy(
        src_ref=warped.at[:, 0:HALO, :], dst_ref=halo.at[1],
        send_sem=halo_send.at[1], recv_sem=halo_recv.at[1], device_id=(sky - 1, me), device_id_type=MESH,
    )

    @pl.when(not_last)
    def _():
        down.start()

    @pl.when(not_first)
    def _():
        up.start()

    def to_peer(src, dst, send_sems, recv_sems, t):
        return pltpu.make_async_remote_copy(
            src_ref=src.at[t - 1], dst_ref=dst.at[t],
            send_sem=send_sems.at[t], recv_sem=recv_sems.at[t], device_id=(sky, peers[t]), device_id_type=MESH,
        )

    v_copies = [to_peer(vsend, vrecv, v_send, v_recv, t) for t in range(1, n_exp)]
    m_copies = [to_peer(msend, mrecv, m_send, m_recv, t) for t in range(1, n_exp)]
    e_copies = [to_peer(esend, erecv, e_send, e_recv, t) for t in range(1, n_exp)]
    for copy in v_copies:
        copy.start()

    small[3].wait()
    small[4].wait()

    def position(row):
        return (2.0 * (sky * ROWS + row).astype(F32) + 1.0) / (n_sky * ROWS) - 1.0

    def coefficients(b, e):
        degree = degrees[e, b]
        return [jnp.where(ORDERS[t] <= degree, coeffs[b, e, t], 0.0) for t in range(10)]

    def cubic(c, u):
        return ((c[6] * u + c[3]) * u + c[1]) * u + c[0], (c[7] * u + c[4]) * u + c[2], c[8] * u + c[5]

    u_lane = position(iota((8, 128), 1))
    i_edge = iota((EDGE, 128), 0)
    u_edge = position(jnp.where(i_edge < LO, i_edge, i_edge + INNER))
    for b in range(NB):
        for e in range(EXPS):
            c = coefficients(b, e)
            gains[b, e, 0], gains[b, e, 1], gains[b, e, 2] = cubic(c, u_lane)
            gains[b, e, 3] = jnp.full((8, 128), c[9], F32)

    for b in range(NB):
        along[b, 0:PAD, :] = jnp.zeros((PAD, 256), BF16)
        along[b, PAD + COLS : COLS + 2 * PAD, :] = jnp.zeros((PAD, 256), BF16)
    own_copy.wait()
    for e in range(EXPS):
        for i in range(COLS // 128):
            span = slice(128 * i, 128 * i + 128)
            block = jnp.concatenate([own[e, :, span].astype(F32), jnp.zeros((128 - ROWS, 128), F32)], axis=0)
            image[e, span, :] = block.T.astype(BF16)

    for e in range(EXPS):
        lanes = slice(128 * e, 128 * e + 128)

        @pl.loop(0, 4)
        def _(n):
            tile = rowband[:, pl.ds(pl.multiple_of(n * 256, 256), 256)]
            filtered = jnp.dot(image[e], tile, preferred_element_type=F32).astype(BF16)
            along[2 * n, PAD : PAD + COLS, lanes] = filtered[:, 0:128]
            along[2 * n + 1, PAD : PAD + COLS, lanes] = filtered[:, 128:256]

        filtered = jnp.dot(image[e], rowband[:, 1024:1152], preferred_element_type=F32).astype(BF16)
        along[8, PAD : PAD + COLS, lanes] = filtered

    def put_interior(ref, j):
        start = pl.multiple_of(j * 128, 128)
        v = (2.0 * (j * 128 + iota((8, 128), 0)).astype(F32) + 1.0) / COLS - 1.0
        first_arg = 2.0 * v + STEP
        second_arg = 3.0 * v * v + 3.0 * STEP * v + STEP * STEP
        third_arg = 3.0 * (v + STEP)
        sums = [[jnp.zeros((8, 128), F32) for _ in range(16)] for _ in range(EXPS)]
        for b in range(NB):
            window = along[b, pl.ds(start, WINDOW), :]
            filtered = jnp.dot(colband[b], window, preferred_element_type=F32)
            for e in range(EXPS):
                g0, g1, g2, g3 = (gains[b, e, q] for q in range(4))
                field = ((g3 * v + g2) * v + g1) * v + g0
                d1 = (g1 + g2 * first_arg + g3 * second_arg) * STEP
                d2 = (g2 + g3 * third_arg) * (2.0 * STEP * STEP)
                d3 = g3 * (6.0 * STEP * STEP * STEP)
                for i in range(16):
                    part = filtered[8 * i : 8 * i + 8, 128 * e : 128 * e + 128]
                    sums[e][i] = sums[e][i] + field * part
                    if i < 15:
                        field = field + d1
                    if i < 14:
                        d1 = d1 + d2
                    if i < 13:
                        d2 = d2 + d3
        for e in range(EXPS):
            ref[e] = jnp.concatenate(sums[e], axis=0).T[LO:HI].astype(BF16)

    for t in range(1, n_exp):
        put_interior(msend.at[t - 1], peers[t])
        m_copies[t - 1].start()

    i_band, kappa = iota((EDGE, 128), 0), iota((EDGE, 128), 1)
    k_edge = (
        jnp.where(kappa < 48, kappa - HALO, kappa + 40) - jnp.where(i_band < LO, i_band, i_band + INNER) + HALF
    )
    k_edge = jnp.where(kappa < EROWS, k_edge, -1)
    k_edge_col = iota((160, 128), 0) + 48 - iota((160, 128), 1) - (64 - HALF)
    for b in range(NB):
        edge_rowband[EDGE * b : EDGE * b + EDGE, :] = band(2 * b, k_edge)[:, 0:EROWS]
        edge_colband[b, 0:48] = jnp.zeros((48, 128), BF16)
        edge_colband[b, 48:208] = band(2 * b + 1, k_edge_col)
        edge_colband[b, 208:256] = jnp.zeros((48, 128), BF16)
        for e in range(EXPS):
            g = cubic(coefficients(b, e), u_edge)
            for q in range(3):
                edge_gains[b, q, EDGE * e : EDGE * e + EDGE, :] = g[q]
    for e in range(EXPS):
        edge_image[e, :, 0:128] = jnp.zeros((EROWS, 128), BF16)
        edge_image[e, :, 1024:1152] = jnp.zeros((EROWS, 128), BF16)
        edge_image[e, 16:48, 64:1088] = own[e, 0:32]
        edge_image[e, 48:80, 64:1088] = own[e, 88:120]

    @pl.when(not_first)
    def _():
        down.wait_recv()

    @pl.when(not_last)
    def _():
        up.wait_recv()

    for e in range(EXPS):
        edge_image[e, 0:16, 64:1088] = halo[0, e]
        edge_image[e, 80:96, 64:1088] = halo[1, e]

    def put_filtered(tile, pieces):
        filtered = jnp.dot(edge_rowband[...], tile, preferred_element_type=F32).astype(BF16)
        for e, span, part in pieces:
            for b in range(NB):
                edge_along[b, EDGE * e : EDGE * e + EDGE, span] = filtered[EDGE * b : EDGE * b + EDGE, part]

    for e in range(EXPS):
        for n in range(4):
            span = slice(256 * n, 256 * n + 256)
            put_filtered(edge_image[e, :, span], [(e, span, slice(0, 256))])
    rest = slice(COLS, COLS + 128)
    put_filtered(
        jnp.concatenate([edge_image[e, :, rest] for e in range(EXPS)], axis=1),
        [(e, rest, slice(128 * e, 128 * e + 128)) for e in range(EXPS)],
    )

    def put_edges(group):
        starts = [pl.multiple_of(peers[t] * 128, 128) for t in group]
        vs = [(2.0 * (peers[t] * 128 + iota((EDGE, 128), 1)).astype(F32) + 1.0) / COLS - 1.0 for t in group]
        sums = [[jnp.zeros((EDGE, 128), F32) for _ in range(EXPS)] for _ in group]
        for b in range(NB):
            windows = jnp.concatenate([edge_along[b, :, pl.ds(s, 256)] for s in starts], axis=0)
            filtered = jnp.dot(windows, edge_colband[b], preferred_element_type=F32)
            for e in range(EXPS):
                g3 = jnp.where(degrees[e, b] >= 3, coeffs[b, e, 9], 0.0)
                g0, g1, g2 = (edge_gains[b, q, EDGE * e : EDGE * e + EDGE, :] for q in range(3))
                for i, v in enumerate(vs):
                    part = filtered[2 * EDGE * i + EDGE * e : 2 * EDGE * i + EDGE * e + EDGE]
                    sums[i][e] = sums[i][e] + (((g3 * v + g2) * v + g1) * v + g0) * part
        for i, t in enumerate(group):
            ref = erecv.at[0] if t == 0 else esend.at[t - 1]
            for e in range(EXPS):
                ref[e] = sums[i][e].astype(BF16)
            if t > 0:
                e_copies[t - 1].start()

    put_edges((1, 2, 3, 4))
    put_edges((5, 6, 7, 0))
    put_interior(mrecv.at[0], peers[0])

    inner_chunks = ((0, 48), (48, INNER))
    for t in range(n_exp):
        if t > 0:
            v_copies[t - 1].wait_recv()
        for e in range(EXPS):
            for lo, hi in ((0, LO), (LO, 64), (64, HI), (HI, ROWS)):
                var = vrecv[t, e, lo:hi].astype(F32)
                weights[t, e, lo:hi] = jnp.where(var > 0.0, 1.0 / var, 0.0)

    def coadd(values, weight_of, shape):
        num, den = jnp.zeros(shape, F32), jnp.zeros(shape, F32)
        for t in range(n_exp):
            for e in range(EXPS):
                weight = weight_of(t, e)
                num = num + weight * values(t, e)
                den = den + weight
        first = num / (1.0 + den)
        num, den = jnp.zeros(shape, F32), jnp.zeros(shape, F32)
        for t in range(n_exp):
            for e in range(EXPS):
                value, weight = values(t, e), weight_of(t, e)
                excess = value - first
                robust = weight / (1.0 + excess * excess * weight * (1.0 / 9.0))
                num = num + robust * value
                den = den + robust
        return num / (1.0 + den)

    for copy in m_copies:
        copy.wait_recv()
    for lo, hi in inner_chunks:
        out[LO + lo : LO + hi, :] = coadd(
            lambda t, e: mrecv[t, e, lo:hi].astype(F32), lambda t, e: weights[t, e, LO + lo : LO + hi], (hi - lo, 128)
        )
    for copy in e_copies:
        copy.wait_recv()
    edges = coadd(
        lambda t, e: erecv[t, e].astype(F32),
        lambda t, e: jnp.concatenate([weights[t, e, 0:LO], weights[t, e, HI:ROWS]], axis=0),
        (EDGE, 128),
    )
    out[0:LO, :] = edges[0:LO]
    out[HI:ROWS, :] = edges[LO:EDGE]

    @pl.when(not_last)
    def _():
        down.wait_send()

    @pl.when(not_first)
    def _():
        up.wait_send()

    for copy in v_copies + m_copies + e_copies:
        copy.wait_send()


def solution(mesh):
    n_sky, n_exp = mesh.shape["sky"], mesh.shape["exp"]

    def body(warped, variance, basis_taps, coeffs, degrees, footprint, masks):
        hbm = pl.BlockSpec(memory_space=pl.ANY)
        vmem = pl.BlockSpec(memory_space=pltpu.VMEM)
        dma = pltpu.SemaphoreType.DMA
        return pl.pallas_call(
            functools.partial(kernel, n_sky, n_exp),
            out_shape=pltpu.VMEM((ROWS, 128), F32),
            in_specs=[hbm] * 7,
            out_specs=vmem,
            scratch_shapes=[
                pltpu.SMEM((NB, EXPS, 10), F32),
                pltpu.SMEM((EXPS, NB), jnp.int32),
                pltpu.SMEM((EXPS, 2), jnp.int32),
                pltpu.SMEM((EXPS, 8), jnp.int32),
                pltpu.VMEM((NB, 2, KW), BF16),
                pltpu.VMEM((EXPS, ROWS, COLS), BF16),
                pltpu.VMEM((2, EXPS, HALO, COLS), BF16),
                pltpu.VMEM((EXPS, ROWS, COLS), BF16),
                pltpu.VMEM((EXPS, COLS, 128), BF16),
                pltpu.VMEM((EXPS, EROWS, COLS + 128), BF16),
                pltpu.VMEM((24, 128), F32),
                pltpu.VMEM((128, NB * 128), BF16),
                pltpu.VMEM((NB, 128, WINDOW), BF16),
                pltpu.VMEM((NB * EDGE, EROWS), BF16),
                pltpu.VMEM((NB, 256, 128), BF16),
                pltpu.VMEM((NB, EXPS, 4, 8, 128), F32),
                pltpu.VMEM((NB, 3, EXPS * EDGE, 128), F32),
                pltpu.VMEM((NB, COLS + 2 * PAD, 256), BF16),
                pltpu.VMEM((NB, EXPS * EDGE, COLS + 128), BF16),
                pltpu.VMEM((n_exp - 1, EXPS, ROWS, 128), BF16),
                pltpu.VMEM((n_exp - 1, EXPS, INNER, 128), BF16),
                pltpu.VMEM((n_exp - 1, EXPS, EDGE, 128), BF16),
                pltpu.VMEM((n_exp, EXPS, ROWS, 128), BF16),
                pltpu.VMEM((n_exp, EXPS, INNER, 128), BF16),
                pltpu.VMEM((n_exp, EXPS, EDGE, 128), BF16),
                pltpu.VMEM((n_exp, EXPS, ROWS, 128), F32),
                dma((5,)), dma((2,)), dma((2,)), dma((2,)),
                dma((n_exp,)), dma((n_exp,)), dma((n_exp,)), dma((n_exp,)), dma((n_exp,)), dma((n_exp,)),
            ],
            compiler_params=pltpu.CompilerParams(
                collective_id=0, has_side_effects=True, vmem_limit_bytes=60 * 1024 * 1024
            ),
            name="coadd",
        )(coeffs.transpose(1, 0, 2), degrees, footprint, masks, basis_taps, warped, variance)

    in_specs = (
        P("exp", "sky", None),
        P("exp", "sky", None),
        P(),
        P("exp", None, None),
        P("exp", None),
        P("exp", None),
        P("exp", "sky"),
    )
    return jax.shard_map(body, mesh=mesh, in_specs=in_specs, out_specs=P("sky", "exp"), check_vma=False)
```

```python
import functools

import jax
import jax.numpy as jnp
from jax import lax
from jax.experimental import pallas as pl
from jax.experimental.pallas import tpu as pltpu
from jax.sharding import PartitionSpec as P

MESH = pl.DeviceIdType.MESH
F32, BF16 = jnp.float32, jnp.bfloat16
EXPS, ROWS, COLS, NB, KW = 2, 120, 1024, 9, 23
HALF = KW // 2
HALO = 16
LO, HI = 16, 104
INNER = HI - LO
EDGE = ROWS - INNER
EROWS = 96
PAD = 16
WINDOW = 160
ORDERS = (0, 1, 1, 2, 2, 2, 3, 3, 3, 3)
STEP = 16.0 / COLS
RING = 4
OFFSETS = ((0, 0), (2, 1), (2, 0), (1, 1), (3, 1), (0, 1), (1, 0), (3, 0))


def iota(shape, dim):
    return lax.broadcasted_iota(jnp.int32, shape, dim)


def kernel(
    n_sky, n_exp, coeffs_hbm, degrees_hbm, footprint_hbm, masks_hbm, taps_hbm, warped, variance, out,
    coeffs, degrees, footprint, masks, taps, own, halo, vraw, image, edge_image, tapbuf, rowband, colband,
    edge_rowband, edge_colband, gains, edge_gains, along, edge_along,
    vsend, msend, esend, vrecv, mrecv, erecv, weights,
    small_sems, local_sems, halo_send, halo_recv, v_send, v_recv, m_send, m_recv, e_send, e_recv,
):
    sky, me = lax.axis_index("sky"), lax.axis_index("exp")
    not_first, not_last = sky > 0, sky < n_sky - 1
    ring, pair = lax.rem(me, RING), me // RING
    peers = [lax.rem(pair + dz, n_exp // RING) * RING + lax.rem(ring + dx, RING) for dx, dz in OFFSETS]

    barrier = pltpu.get_barrier_semaphore()

    @pl.when(not_last)
    def _():
        pl.semaphore_signal(barrier, inc=1, device_id=(sky + 1, me), device_id_type=MESH)

    @pl.when(not_first)
    def _():
        pl.semaphore_signal(barrier, inc=1, device_id=(sky - 1, me), device_id_type=MESH)

    for t in range(1, n_exp):
        pl.semaphore_signal(barrier, inc=1, device_id=(sky, peers[t]), device_id_type=MESH)

    small = [
        pltpu.make_async_copy(src, dst, small_sems.at[i])
        for i, (src, dst) in enumerate((
            (taps_hbm, taps), (masks_hbm, masks), (footprint_hbm, footprint), (coeffs_hbm, coeffs), (degrees_hbm, degrees),
        ))
    ]
    for copy in small:
        copy.start()
    var_copy = pltpu.make_async_copy(variance, vraw, local_sems.at[0])
    own_copy = pltpu.make_async_copy(warped, own, local_sems.at[1])
    var_copy.start()
    own_copy.start()

    @pl.when(jnp.logical_not(not_first))
    def _():
        halo[0] = jnp.zeros((EXPS, HALO, COLS), BF16)

    @pl.when(jnp.logical_not(not_last))
    def _():
        halo[1] = jnp.zeros((EXPS, HALO, COLS), BF16)

    tapbuf[...] = jnp.zeros_like(tapbuf)
    small[0].wait()
    for b in range(NB):
        tapbuf[2 * b : 2 * b + 2, 0:KW] = taps[b].astype(F32)

    def band(row, k):
        table = jnp.broadcast_to(tapbuf[row : row + 1, :], k.shape)
        picked = jnp.take_along_axis(table, jnp.clip(k, 0, 127), axis=1)
        return jnp.where((k >= 0) & (k < KW), picked, 0.0).astype(BF16)

    low, lane = iota((128, 128), 0), iota((128, 128), 1)
    k_row = jnp.where(low < ROWS, low - lane + HALF, -1)
    k_first = lane - low - (PAD - HALF)
    k_second = k_first + 128
    tail = 96
    for b in range(NB):
        rowband[:, 128 * b : 128 * b + 128] = band(2 * b, k_row)
        colband[b, :, 0:128] = band(2 * b + 1, k_first)
        colband[b, 0:tail, 128:WINDOW] = jnp.zeros((tail, WINDOW - 128), BF16)
        colband[b, tail:128, 128:WINDOW] = band(2 * b + 1, k_second[tail:128])[:, 0 : WINDOW - 128]

    small[1].wait()
    small[2].wait()
    var_copy.wait()
    rows = iota((ROWS, 128), 0)
    word_at = (rows * 137) >> 11
    offset = 2 * (rows - 15 * word_at)
    global_row = sky * ROWS + rows
    for e in range(EXPS):
        word = jnp.zeros((ROWS, 128), jnp.int32)
        for i in range(ROWS // 15):
            word = jnp.where(word_at == i, masks[e, i], word)
        usable = (
            (((word >> offset) & 3) != 3)
            & (global_row >= footprint[e, 0])
            & (global_row < footprint[e, 1])
        )
        for t in range(n_exp):
            block = vraw[e, :, pl.ds(pl.multiple_of(peers[t] * 128, 128), 128)].astype(F32)
            masked = jnp.where(usable, block, 0.0).astype(BF16)
            if t == 0:
                vrecv[0, e] = masked
            else:
                vsend[t - 1, e] = masked

    own_copy.wait()
    n_neighbours = not_first.astype(jnp.int32) + not_last.astype(jnp.int32)
    pl.semaphore_wait(barrier, n_exp - 1 + n_neighbours)

    down = pltpu.make_async_remote_copy(
        src_ref=own.at[:, ROWS - HALO : ROWS, :], dst_ref=halo.at[0],
        send_sem=halo_send.at[0], recv_sem=halo_recv.at[0], device_id=(sky + 1, me), device_id_type=MESH,
    )
    up = pltpu.make_async_remote_copy(
        src_ref=own.at[:, 0:HALO, :], dst_ref=halo.at[1],
        send_sem=halo_send.at[1], recv_sem=halo_recv.at[1], device_id=(sky - 1, me), device_id_type=MESH,
    )

    @pl.when(not_last)
    def _():
        down.start()

    @pl.when(not_first)
    def _():
        up.start()

    def to_peer(src, dst, send_sems, recv_sems, t):
        return pltpu.make_async_remote_copy(
            src_ref=src.at[t - 1], dst_ref=dst.at[t],
            send_sem=send_sems.at[t], recv_sem=recv_sems.at[t], device_id=(sky, peers[t]), device_id_type=MESH,
        )

    v_copies = [to_peer(vsend, vrecv, v_send, v_recv, t) for t in range(1, n_exp)]
    m_copies = [to_peer(msend, mrecv, m_send, m_recv, t) for t in range(1, n_exp)]
    e_copies = [to_peer(esend, erecv, e_send, e_recv, t) for t in range(1, n_exp)]
    for copy in v_copies:
        copy.start()

    small[3].wait()
    small[4].wait()

    def position(row):
        return (2.0 * (sky * ROWS + row).astype(F32) + 1.0) / (n_sky * ROWS) - 1.0

    def coefficients(b, e):
        degree = degrees[e, b]
        return [jnp.where(ORDERS[t] <= degree, coeffs[b, e, t], 0.0) for t in range(10)]

    def cubic(c, u):
        return ((c[6] * u + c[3]) * u + c[1]) * u + c[0], (c[7] * u + c[4]) * u + c[2], c[8] * u + c[5]

    u_lane = position(iota((8, 128), 1))
    i_edge = iota((EDGE, 128), 0)
    u_edge = position(jnp.where(i_edge < LO, i_edge, i_edge + INNER))
    for b in range(NB):
        for e in range(EXPS):
            c = coefficients(b, e)
            gains[b, e, 0], gains[b, e, 1], gains[b, e, 2] = cubic(c, u_lane)
            gains[b, e, 3] = jnp.full((8, 128), c[9], F32)

    for b in range(NB):
        along[b, 0:PAD, :] = jnp.zeros((PAD, 256), BF16)
        along[b, PAD + COLS : COLS + 2 * PAD, :] = jnp.zeros((PAD, 256), BF16)
    for e in range(EXPS):
        for i in range(COLS // 128):
            span = slice(128 * i, 128 * i + 128)
            block = jnp.concatenate([own[e, :, span].astype(F32), jnp.zeros((128 - ROWS, 128), F32)], axis=0)
            image[e, span, :] = block.T.astype(BF16)

    for e in range(EXPS):
        lanes = slice(128 * e, 128 * e + 128)

        @pl.loop(0, 4)
        def _(n):
            tile = rowband[:, pl.ds(pl.multiple_of(n * 256, 256), 256)]
            filtered = jnp.dot(image[e], tile, preferred_element_type=F32).astype(BF16)
            along[2 * n, PAD : PAD + COLS, lanes] = filtered[:, 0:128]
            along[2 * n + 1, PAD : PAD + COLS, lanes] = filtered[:, 128:256]

        filtered = jnp.dot(image[e], rowband[:, 1024:1152], preferred_element_type=F32).astype(BF16)
        along[8, PAD : PAD + COLS, lanes] = filtered

    def put_interior(ref, j):
        start = pl.multiple_of(j * 128, 128)
        v = (2.0 * (j * 128 + iota((8, 128), 0)).astype(F32) + 1.0) / COLS - 1.0
        first_arg = 2.0 * v + STEP
        second_arg = 3.0 * v * v + 3.0 * STEP * v + STEP * STEP
        third_arg = 3.0 * (v + STEP)
        sums = [[jnp.zeros((8, 128), F32) for _ in range(16)] for _ in range(EXPS)]
        for b in range(NB):
            window = along[b, pl.ds(start, WINDOW), :]
            filtered = jnp.dot(colband[b], window, preferred_element_type=F32)
            for e in range(EXPS):
                g0, g1, g2, g3 = (gains[b, e, q] for q in range(4))
                field = ((g3 * v + g2) * v + g1) * v + g0
                d1 = (g1 + g2 * first_arg + g3 * second_arg) * STEP
                d2 = (g2 + g3 * third_arg) * (2.0 * STEP * STEP)
                d3 = g3 * (6.0 * STEP * STEP * STEP)
                for i in range(16):
                    part = filtered[8 * i : 8 * i + 8, 128 * e : 128 * e + 128]
                    sums[e][i] = sums[e][i] + field * part
                    if i < 15:
                        field = field + d1
                    if i < 14:
                        d1 = d1 + d2
                    if i < 13:
                        d2 = d2 + d3
        for e in range(EXPS):
            ref[e] = jnp.concatenate(sums[e], axis=0).T[LO:HI].astype(BF16)

    for t in range(1, n_exp):
        put_interior(msend.at[t - 1], peers[t])
        m_copies[t - 1].start()

    i_band, kappa = iota((EDGE, 128), 0), iota((EDGE, 128), 1)
    k_edge = (
        jnp.where(kappa < 48, kappa - HALO, kappa + 40) - jnp.where(i_band < LO, i_band, i_band + INNER) + HALF
    )
    k_edge = jnp.where(kappa < EROWS, k_edge, -1)
    k_edge_col = iota((160, 128), 0) + 48 - iota((160, 128), 1) - (64 - HALF)
    for b in range(NB):
        edge_rowband[EDGE * b : EDGE * b + EDGE, :] = band(2 * b, k_edge)[:, 0:EROWS]
        edge_colband[b, 0:48] = jnp.zeros((48, 128), BF16)
        edge_colband[b, 48:208] = band(2 * b + 1, k_edge_col)
        edge_colband[b, 208:256] = jnp.zeros((48, 128), BF16)
        for e in range(EXPS):
            g = cubic(coefficients(b, e), u_edge)
            for q in range(3):
                edge_gains[b, q, EDGE * e : EDGE * e + EDGE, :] = g[q]
    for e in range(EXPS):
        edge_image[e, :, 0:128] = jnp.zeros((EROWS, 128), BF16)
        edge_image[e, :, 1024:1152] = jnp.zeros((EROWS, 128), BF16)
        edge_image[e, 16:48, 64:1088] = own[e, 0:32]
        edge_image[e, 48:80, 64:1088] = own[e, 88:120]

    @pl.when(not_first)
    def _():
        down.wait_recv()

    @pl.when(not_last)
    def _():
        up.wait_recv()

    for e in range(EXPS):
        edge_image[e, 0:16, 64:1088] = halo[0, e]
        edge_image[e, 80:96, 64:1088] = halo[1, e]

    def put_filtered(tile, pieces):
        filtered = jnp.dot(edge_rowband[...], tile, preferred_element_type=F32).astype(BF16)
        for e, span, part in pieces:
            for b in range(NB):
                edge_along[b, EDGE * e : EDGE * e + EDGE, span] = filtered[EDGE * b : EDGE * b + EDGE, part]

    for e in range(EXPS):
        for n in range(4):
            span = slice(256 * n, 256 * n + 256)
            put_filtered(edge_image[e, :, span], [(e, span, slice(0, 256))])
    rest = slice(COLS, COLS + 128)
    put_filtered(
        jnp.concatenate([edge_image[e, :, rest] for e in range(EXPS)], axis=1),
        [(e, rest, slice(128 * e, 128 * e + 128)) for e in range(EXPS)],
    )

    def put_edges(group):
        starts = [pl.multiple_of(peers[t] * 128, 128) for t in group]
        vs = [(2.0 * (peers[t] * 128 + iota((EDGE, 128), 1)).astype(F32) + 1.0) / COLS - 1.0 for t in group]
        sums = [[jnp.zeros((EDGE, 128), F32) for _ in range(EXPS)] for _ in group]
        for b in range(NB):
            windows = jnp.concatenate([edge_along[b, :, pl.ds(s, 256)] for s in starts], axis=0)
            filtered = jnp.dot(windows, edge_colband[b], preferred_element_type=F32)
            for e in range(EXPS):
                g3 = jnp.where(degrees[e, b] >= 3, coeffs[b, e, 9], 0.0)
                g0, g1, g2 = (edge_gains[b, q, EDGE * e : EDGE * e + EDGE, :] for q in range(3))
                for i, v in enumerate(vs):
                    part = filtered[2 * EDGE * i + EDGE * e : 2 * EDGE * i + EDGE * e + EDGE]
                    sums[i][e] = sums[i][e] + (((g3 * v + g2) * v + g1) * v + g0) * part
        for i, t in enumerate(group):
            ref = erecv.at[0] if t == 0 else esend.at[t - 1]
            for e in range(EXPS):
                ref[e] = sums[i][e].astype(BF16)
            if t > 0:
                e_copies[t - 1].start()

    put_edges((1, 2, 3, 4))
    put_edges((5, 6, 7, 0))
    put_interior(mrecv.at[0], peers[0])

    inner_chunks = ((0, 48), (48, INNER))
    for t in range(n_exp):
        if t > 0:
            v_copies[t - 1].wait_recv()
        for e in range(EXPS):
            for lo, hi in ((0, LO), (LO, 64), (64, HI), (HI, ROWS)):
                var = vrecv[t, e, lo:hi].astype(F32)
                weights[t, e, lo:hi] = jnp.where(var > 0.0, 1.0 / var, 0.0)

    def coadd(values, weight_of, shape):
        num, den = jnp.zeros(shape, F32), jnp.zeros(shape, F32)
        for t in range(n_exp):
            for e in range(EXPS):
                weight = weight_of(t, e)
                num = num + weight * values(t, e)
                den = den + weight
        first = num / (1.0 + den)
        num, den = jnp.zeros(shape, F32), jnp.zeros(shape, F32)
        for t in range(n_exp):
            for e in range(EXPS):
                value, weight = values(t, e), weight_of(t, e)
                excess = value - first
                robust = weight / (1.0 + excess * excess * weight * (1.0 / 9.0))
                num = num + robust * value
                den = den + robust
        return num / (1.0 + den)

    for copy in m_copies:
        copy.wait_recv()
    for lo, hi in inner_chunks:
        out[LO + lo : LO + hi, :] = coadd(
            lambda t, e: mrecv[t, e, lo:hi].astype(F32), lambda t, e: weights[t, e, LO + lo : LO + hi], (hi - lo, 128)
        )
    for copy in e_copies:
        copy.wait_recv()
    edges = coadd(
        lambda t, e: erecv[t, e].astype(F32),
        lambda t, e: jnp.concatenate([weights[t, e, 0:LO], weights[t, e, HI:ROWS]], axis=0),
        (EDGE, 128),
    )
    out[0:LO, :] = edges[0:LO]
    out[HI:ROWS, :] = edges[LO:EDGE]

    @pl.when(not_last)
    def _():
        down.wait_send()

    @pl.when(not_first)
    def _():
        up.wait_send()

    for copy in v_copies + m_copies + e_copies:
        copy.wait_send()


def solution(mesh):
    n_sky, n_exp = mesh.shape["sky"], mesh.shape["exp"]

    def body(warped, variance, basis_taps, coeffs, degrees, footprint, masks):
        hbm = pl.BlockSpec(memory_space=pl.ANY)
        vmem = pl.BlockSpec(memory_space=pltpu.VMEM)
        dma = pltpu.SemaphoreType.DMA
        return pl.pallas_call(
            functools.partial(kernel, n_sky, n_exp),
            out_shape=pltpu.VMEM((ROWS, 128), F32),
            in_specs=[hbm] * 7,
            out_specs=vmem,
            scratch_shapes=[
                pltpu.SMEM((NB, EXPS, 10), F32),
                pltpu.SMEM((EXPS, NB), jnp.int32),
                pltpu.SMEM((EXPS, 2), jnp.int32),
                pltpu.SMEM((EXPS, 8), jnp.int32),
                pltpu.VMEM((NB, 2, KW), BF16),
                pltpu.VMEM((EXPS, ROWS, COLS), BF16),
                pltpu.VMEM((2, EXPS, HALO, COLS), BF16),
                pltpu.VMEM((EXPS, ROWS, COLS), BF16),
                pltpu.VMEM((EXPS, COLS, 128), BF16),
                pltpu.VMEM((EXPS, EROWS, COLS + 128), BF16),
                pltpu.VMEM((24, 128), F32),
                pltpu.VMEM((128, NB * 128), BF16),
                pltpu.VMEM((NB, 128, WINDOW), BF16),
                pltpu.VMEM((NB * EDGE, EROWS), BF16),
                pltpu.VMEM((NB, 256, 128), BF16),
                pltpu.VMEM((NB, EXPS, 4, 8, 128), F32),
                pltpu.VMEM((NB, 3, EXPS * EDGE, 128), F32),
                pltpu.VMEM((NB, COLS + 2 * PAD, 256), BF16),
                pltpu.VMEM((NB, EXPS * EDGE, COLS + 128), BF16),
                pltpu.VMEM((n_exp - 1, EXPS, ROWS, 128), BF16),
                pltpu.VMEM((n_exp - 1, EXPS, INNER, 128), BF16),
                pltpu.VMEM((n_exp - 1, EXPS, EDGE, 128), BF16),
                pltpu.VMEM((n_exp, EXPS, ROWS, 128), BF16),
                pltpu.VMEM((n_exp, EXPS, INNER, 128), BF16),
                pltpu.VMEM((n_exp, EXPS, EDGE, 128), BF16),
                pltpu.VMEM((n_exp, EXPS, ROWS, 128), F32),
                dma((5,)), dma((2,)), dma((2,)), dma((2,)),
                dma((n_exp,)), dma((n_exp,)), dma((n_exp,)), dma((n_exp,)), dma((n_exp,)), dma((n_exp,)),
            ],
            compiler_params=pltpu.CompilerParams(
                collective_id=0, has_side_effects=True, vmem_limit_bytes=60 * 1024 * 1024
            ),
            name="coadd",
        )(coeffs.transpose(1, 0, 2), degrees, footprint, masks, basis_taps, warped, variance)

    in_specs = (
        P("exp", "sky", None),
        P("exp", "sky", None),
        P(),
        P("exp", None, None),
        P("exp", None),
        P("exp", None),
        P("exp", "sky"),
    )
    return jax.shard_map(body, mesh=mesh, in_specs=in_specs, out_specs=P("sky", "exp"), check_vma=False)
```
